128 devices in a mesh: row: 8 (over x, z_hi), col: 16 (over y, z_lo, core).
Axes of the slice: x: 4, y: 4, z: 4 (z_hi: 2, z_lo: 2; z = z_hi * 2 + z_lo), core: 2. Of those that a mesh axis runs over, the one named last changes fastest.
Arguments:
- points: float32 [8, 131072], P(None, ('row', 'col')), may hold values from -4 to 4
- point_order: int32 [128, 1024], P(('row', 'col')), may hold values from 0 to 1023, each once within a row
- noise_var: float32 [131072], P(('row', 'col')), may hold values from 0.1 to 3
- inv_scale: float32 [8], replicated, may hold values from 0.2 to 0.6
- basis_vectors: float32 [16, 64, 131072], P(None, None, ('row', 'col')), may hold values from -4 to 4
- current: float32 [64, 131072], P(None, ('row', 'col')), may hold values from -22 to 22
- tile_rows: int32 [8, 16, 64], P('row', 'col'), may hold values from 0 to 63, as said below
- tile_cols: int32 [8, 16, 64], P('row', 'col'), may hold values from 0 to 31
Outputs:
- lanczos_next: float32 [64, 131072], P(None, ('row', 'col'))
- coefficients: float32 [4, 64], replicated
- gradient_product: float32 [64, 131072], P(None, ('row', 'col'))
The draws below stay inside these ranges and needn't reach their ends.
Inputs may be any that keep to these rules, and one draw needn't show every extreme that they name: In each grid cell the 64 pairs (tile_rows, tile_cols) are distinct; each cell lists its 4 pairs with I = J; over all cells no unordered pair of distinct blocks is listed twice: it is listed as (I, J) with I < J when I + J is odd and with I > J when I + J is even.
All inputs are finite; a program needn't handle non-finite values.
Results may differ from the reference program's by a relative error of at most 0.00019.
Values sent between devices are 32-bit elements; how exact they have to be, the bound alone decides.
No kernel may reach another device: no remote copies, remote signals or barrier semaphores. Data moves between devices by JAX's collectives and lax.ppermute only.
A program may use at most 128 MiB of HBM per device.

```python
import math
import jax
import jax.numpy as jnp
from jax import lax

FEAT = 8
BLOCK = 256
PROBES = 64
HISTORY = 16
ITERS = 2
PTS_DEV = 1024
BLOCKS_DEV = 4
TILES = 64
SPANS = 128
POINTS = 131072
ROW_BLOCKS = 64
COL_BLOCKS = 32
N_ROW = 8
N_COL = 16


def window_vectors(key):
    shared = jax.random.fold_in(key, 41)
    ramp_up = 1.0 + 2.0 * jnp.arange(POINTS, dtype=jnp.float32) / POINTS
    stored = jnp.clip(jax.random.normal(jax.random.fold_in(shared, 4), (HISTORY, PROBES, POINTS), jnp.float32), -4.0, 4.0)
    fresh_part = jnp.clip(jax.random.normal(jax.random.fold_in(shared, 5), (PROBES, POINTS), jnp.float32), -4.0, 4.0)
    mixture = (fresh_part + 0.4 * stored[HISTORY - 1] + 0.4 * stored[HISTORY - 2]) * ramp_up
    return (stored, mixture)


def draw_basis_vectors(key, part):
    return window_vectors(key)[0]


def draw_current(key, part):
    return window_vectors(key)[1]


def tile_pattern(key):
    pattern_key = jax.random.fold_in(key, 5)
    slot_count = ROW_BLOCKS * COL_BLOCKS
    slot_ids = jnp.arange(slot_count, dtype=jnp.int32)
    local_row = slot_ids // COL_BLOCKS
    local_col = slot_ids % COL_BLOCKS
    row_index = jnp.arange(N_ROW, dtype=jnp.int32)[:, None, None]
    col_index = jnp.arange(N_COL, dtype=jnp.int32)[None, :, None]
    global_row = row_index * ROW_BLOCKS + local_row[None, None, :]
    global_col = (local_col[None, None, :] // BLOCKS_DEV * N_COL + col_index) * BLOCKS_DEV + local_col[None, None, :] % BLOCKS_DEV
    odd_sum = (global_row + global_col) % 2 == 1
    diagonal = global_row == global_col
    stored = diagonal | ((global_row < global_col) == odd_sum)
    open_slot = stored & jnp.logical_not(diagonal)
    random_part = jax.random.randint(pattern_key, (N_ROW, N_COL, slot_count), 0, 4096, jnp.int32)
    base_rank = random_part * slot_count + slot_ids
    boosted = jnp.zeros(base_rank.shape, jnp.bool_)
    for line_mask in (local_row == 0, local_row == ROW_BLOCKS - 1, local_col == 0, local_col == COL_BLOCKS - 1):
        masked = jnp.where(line_mask[None, None, :] & open_slot, base_rank, -1 - slot_ids)
        best_slot = lax.top_k(masked, 1)[1]
        reached = jnp.take_along_axis(masked, best_slot, axis=2) >= 0
        boosted = boosted | (slot_ids == best_slot) & reached
    tier_level = jnp.where(diagonal, 3, jnp.where(boosted, 2, jnp.where(stored, 1, 0)))
    priority = tier_level * (4096 * slot_count) + base_rank
    chosen = lax.top_k(priority, TILES)[1]
    return ((chosen // COL_BLOCKS).astype(jnp.int32), (chosen % COL_BLOCKS).astype(jnp.int32))


def draw_tile_rows(key, part):
    return tile_pattern(key)[0]


def draw_tile_cols(key, part):
    return tile_pattern(key)[1]


def block_levels(own_key, dims, pieces, least, top_value):
    def one(axis_at, shards_of):
        draws = jax.random.uniform(jax.random.fold_in(jax.random.fold_in(own_key, 6), axis_at), (shards_of,), jnp.float32, least / len(pieces), top_value / len(pieces))
        return jnp.repeat(jnp.exp(draws), dims[axis_at] // shards_of).reshape((-1,) + (1,) * (len(dims) - axis_at - 1))

    loudness = one(*pieces[0])
    for cut in pieces[1:]:
        loudness = loudness * one(*cut)
    return loudness


def noise(own_key, shape, width, limit, pieces=(), kind=jnp.bfloat16):
    factor_of = block_levels(own_key, shape, pieces, -0.22, 0.18) if pieces else 1.0
    result = jax.random.normal(own_key, shape, jnp.float32) * width * factor_of
    return jnp.minimum(jnp.maximum(result, -limit), limit).astype(kind)


def setup_inputs(seed: int = 0) -> dict:
    seeds = jax.random.split(jax.random.key(seed), 9)
    points = noise(seeds[0], (FEAT, POINTS), 1.0, 4.0, ((1, 128),), jnp.float32)
    point_order = jax.vmap(lambda own: jax.random.permutation(own, PTS_DEV))(jax.random.split(seeds[1], SPANS)).reshape((SPANS, PTS_DEV)).astype(jnp.int32)
    noise_var = jnp.clip(jnp.exp(math.log(3.0) - 3.4011974 * jax.random.uniform(seeds[2], (POINTS,), jnp.float32) ** block_levels(seeds[2], (POINTS,), ((0, 128),), -0.2, 0.2)), 0.1, 3.0)
    inv_scale = jnp.clip(jnp.exp(jax.random.uniform(seeds[3], (FEAT,), jnp.float32, math.log(0.2), math.log(0.6))), 0.2, 0.6)
    basis_vectors = draw_basis_vectors(jax.random.fold_in(seeds[8], 71), 0)
    current = draw_current(jax.random.fold_in(seeds[8], 71), 0)
    tile_rows = draw_tile_rows(jax.random.fold_in(seeds[8], 71), 0)
    tile_cols = draw_tile_cols(jax.random.fold_in(seeds[8], 71), 0)
    return dict(points=points, point_order=point_order, noise_var=noise_var, inv_scale=inv_scale, basis_vectors=basis_vectors, current=current, tile_rows=tile_rows, tile_cols=tile_cols)


ROOT_THREE = math.sqrt(3.0)
SUPPORT = 3.0
EPSILON = 1e-06
HIGHEST = lax.Precision.HIGHEST

def kernel_tiles(row_points, col_points):
    dist_sq = jnp.zeros((row_points.shape[1], row_points.shape[2], col_points.shape[2]), jnp.float32)
    for feature in range(row_points.shape[0]):
        differ = row_points[feature][:, :, None] - col_points[feature][:, None, :]
        dist_sq = dist_sq + differ * differ
    shifted = dist_sq + EPSILON
    radius = jnp.sqrt(shifted)
    decaying = jnp.exp(-ROOT_THREE * radius)
    matern_part = (1.0 + ROOT_THREE * radius) * decaying
    tapered = jnp.maximum(1.0 - radius / SUPPORT, 0.0)
    taper_cube = tapered * tapered * tapered
    weight = taper_cube * tapered * (1.0 + 4.0 * radius / SUPPORT)
    kernel_tile = matern_part * weight
    slope_tile = shifted * (3.0 * decaying * weight + 20.0 * matern_part * taper_cube / (SUPPORT * SUPPORT))
    return (kernel_tile, slope_tile)

def operate(values, block_points, row_list, col_list, mirror_list, with_slope):
    probe_count = values.shape[0]
    blocked = values.reshape(probe_count, -1, BLOCK)
    layers = 2 if with_slope else 1
    group_size = math.gcd(row_list.shape[0], 8)
    grouped = (row_list.reshape(-1, group_size), col_list.reshape(-1, group_size), mirror_list.reshape(-1, group_size))

    def one_group(totals, listed):
        row_pick, col_pick, mirror_pick = listed
        kernel_tile, slope_tile = kernel_tiles(jnp.take(block_points, row_pick, axis=1), jnp.take(block_points, col_pick, axis=1))
        if with_slope:
            stacked = jnp.stack([kernel_tile, slope_tile])
        else:
            stacked = kernel_tile[None]
        col_side = jnp.take(blocked, col_pick, axis=1)
        row_side = jnp.take(blocked, row_pick, axis=1) * mirror_pick[None, :, None]
        direct = jnp.einsum('pgj,kgij->kpgi', col_side, stacked, precision=HIGHEST)
        mirrored = jnp.einsum('pgi,kgij->kpgj', row_side, stacked, precision=HIGHEST)
        totals = totals.at[:, :, row_pick].add(direct)
        totals = totals.at[:, :, col_pick].add(mirrored)
        return (totals, None)
    totals = jnp.zeros((layers, probe_count, blocked.shape[1], BLOCK), jnp.float32)
    totals, unused = lax.scan(one_group, totals, grouped)
    return totals.reshape(layers, probe_count, -1)

def reference(points, point_order, noise_var, inv_scale, basis_vectors, current, tile_rows, tile_cols):
    offsets = (jnp.arange(SPANS, dtype=jnp.int32) * PTS_DEV)[:, None]
    arrangement = (point_order + offsets).reshape(-1).astype(jnp.int32)
    scaled = jnp.take(points, arrangement, axis=1) * inv_scale[:, None]
    noise_arranged = jnp.take(noise_var, arrangement)
    block_points = scaled.reshape(FEAT, -1, BLOCK)
    row_index = jnp.arange(N_ROW, dtype=jnp.int32)[:, None, None]
    col_index = jnp.arange(N_COL, dtype=jnp.int32)[None, :, None]
    global_row = (row_index * ROW_BLOCKS + tile_rows).reshape(-1).astype(jnp.int32)
    global_col = ((tile_cols // BLOCKS_DEV * N_COL + col_index) * BLOCKS_DEV + tile_cols % BLOCKS_DEV).reshape(-1).astype(jnp.int32)
    mirror_list = (global_row != global_col).astype(jnp.float32)
    earlier = basis_vectors
    coefficient_rows = []
    gradient_product = current
    for iteration in range(ITERS):
        images = operate(current, block_points, global_row, global_col, mirror_list, iteration == 0)
        if iteration == 0:
            gradient_product = images[1]
        image_vec = images[0] + noise_arranged * current
        earlier_dots = jnp.einsum('hpn,pn->hp', earlier, image_vec, precision=HIGHEST) / POINTS
        alpha_now = lax.optimization_barrier(jnp.sum(current * image_vec, axis=1)) / POINTS
        residual_vec = image_vec - alpha_now[:, None] * current - jnp.einsum('hp,hpn->pn', earlier_dots, earlier, precision=HIGHEST)
        beta_now = jnp.sqrt(lax.optimization_barrier(jnp.sum(residual_vec * residual_vec, axis=1)) / POINTS + EPSILON)
        coefficient_rows += [alpha_now, beta_now]
        if iteration + 1 < ITERS:
            earlier = jnp.concatenate([earlier, current[None]], axis=0)
        current = residual_vec / beta_now[:, None]
    return (current, jnp.stack(coefficient_rows), gradient_product)
```

```python
import functools
import math

import jax
import jax.numpy as jnp
from jax import lax
from jax.experimental import pallas as pl
from jax.experimental.pallas import tpu as pltpu
from jax.sharding import PartitionSpec as P

BLOCK = 256
ITERS = 2
GROUP = 4

ROOT_THREE = math.sqrt(3.0)
SUPPORT = 3.0
EPSILON = 1e-06
HIGHEST = lax.Precision.HIGHEST
F32 = jnp.float32
BF16 = jnp.bfloat16


def shift_y(v, s):
    return lax.ppermute(v, "col", [(i, (i + 4 * s) % 16) for i in range(16)])


def shift_x(v, s):
    return lax.ppermute(v, "row", [(i, (i + 2 * s) % 8) for i in range(8)])


def flip_core(v):
    return lax.ppermute(v, "col", [(i, i ^ 1) for i in range(16)])


def flip_z_lo(v):
    return lax.ppermute(v, "col", [(i, i ^ 2) for i in range(16)])


def flip_z_hi(v):
    return lax.ppermute(v, "row", [(i, i ^ 1) for i in range(8)])


def sum_everywhere(v):
    for axis, size, bits in (("col", 16, (1, 2, 4, 8)), ("row", 8, (1, 2, 4))):
        for bit in bits:
            v = v + lax.ppermute(v, axis, [(i, i ^ bit) for i in range(size)])
    return v


def gather_row_group(v):
    pair = jnp.stack([v, flip_z_hi(v)])
    return [pair] + [shift_x(pair, s) for s in (1, 2, 3)]


def gather_col_group(v):
    pair = jnp.stack([v, flip_z_lo(v)])
    own = [pair] + [shift_y(pair, s) for s in (1, 2, 3)]
    return own + [flip_core(v) for v in own]


def split_three(v):
    high = v.astype(BF16).astype(F32)
    rest = v - high
    middle = rest.astype(BF16).astype(F32)
    return high, middle, rest - middle


def tile_kernel(row_at, col_at, row_points, col_points, scale, kern, slope, left, right):
    @pl.when(pl.program_id(0) == 0)
    def _():
        def features(points, is_left):
            scaled = points * scale[...]
            size = scaled.shape[1]
            norm = split_three(jnp.sum(scaled * scaled, axis=0, keepdims=True))
            one = jnp.ones((1, size), F32)
            none = jnp.zeros((2, size), F32)
            if is_left:
                high, middle, low = split_three(scaled)
                parts = [high, high, middle, middle, high, low, *norm, one, one, one]
            else:
                high, middle, low = split_three(-2.0 * scaled)
                parts = [high, middle, high, middle, low, high, one, one, one, *norm]
            parts += [none, jnp.zeros((8, size), F32)]
            return jnp.concatenate(parts, axis=0).astype(BF16)

        width = 1024
        for k in range(row_points.shape[1] // width):
            at = pl.ds(k * width, width)
            left[:, at] = features(row_points[:, at], True)
        for k in range(col_points.shape[1] // width):
            at = pl.ds(k * width, width)
            right[:, at] = features(col_points[:, at], False)

    base = pl.program_id(0) * GROUP
    for g in range(GROUP):
        row_lane = pl.multiple_of(row_at[base + g], BLOCK)
        col_lane = pl.multiple_of(col_at[base + g], BLOCK)
        dist_sq = lax.dot_general(
            left[:, pl.ds(row_lane, BLOCK)],
            right[:, pl.ds(col_lane, BLOCK)],
            (((0,), (0,)), ((), ())),
            preferred_element_type=F32,
        )
        shifted = jnp.maximum(dist_sq, 0.0) + EPSILON
        radius = shifted * lax.rsqrt(shifted)
        decaying = jnp.exp(-ROOT_THREE * radius)
        growing = 1.0 + ROOT_THREE * radius
        tapered = jnp.maximum(1.0 - radius * (1.0 / SUPPORT), 0.0)
        common = decaying * (tapered * tapered * tapered)
        weight = tapered * (1.0 + (4.0 / SUPPORT) * radius)
        kernel_tile = common * weight * growing
        slope_tile = shifted * common * (3.0 * weight + (20.0 / (SUPPORT * SUPPORT)) * growing)
        for out, tile in ((kern, kernel_tile), (slope, slope_tile)):
            high = tile.astype(BF16)
            out[g, 0] = high
            out[g, 1] = (tile - high.astype(F32)).astype(BF16)


def make_tiles(row_at, col_at, row_points, col_points, scale):
    tiles = row_at.shape[0]
    whole = lambda v: pl.BlockSpec(v.shape, lambda i, *_: (0,) * v.ndim)
    out_spec = pl.BlockSpec((GROUP, 2, BLOCK, BLOCK), lambda i, *_: (i, 0, 0, 0))
    out = jax.ShapeDtypeStruct((tiles, 2, BLOCK, BLOCK), BF16)
    return pl.pallas_call(
        tile_kernel,
        out_shape=(out, out),
        grid_spec=pltpu.PrefetchScalarGridSpec(
            num_scalar_prefetch=2,
            grid=(tiles // GROUP,),
            in_specs=[whole(row_points), whole(col_points), whole(scale)],
            out_specs=(out_spec, out_spec),
            scratch_shapes=[
                pltpu.VMEM((64, row_points.shape[1]), BF16),
                pltpu.VMEM((64, col_points.shape[1]), BF16),
            ],
        ),
        compiler_params=pltpu.CompilerParams(vmem_limit_bytes=32 << 20),
        cost_estimate=pl.CostEstimate(
            flops=tiles * 30 * BLOCK * BLOCK,
            bytes_accessed=tiles * 8 * BLOCK * BLOCK,
            transcendentals=tiles * 2 * BLOCK * BLOCK,
        ),
        name="make_tiles",
    )(row_at, col_at, row_points, col_points, scale)


def product_kernel(row_count, col_count, flat, index, tiles, *refs):
    row_in, refs = refs[:row_count], refs[row_count:]
    col_in, refs = refs[:col_count], refs[col_count:]
    if flat:
        row_out, col_out = [refs[0]], [refs[1]]
        refs = refs[2:]
    else:
        row_out, col_out, refs = refs[:2], refs[2:6], refs[6:]
    row_held, col_held, row_total, col_total = refs
    step = pl.program_id(0)

    @pl.when(step == 0)
    def _():
        def hold(held, arrays):
            slot = 0
            for array in arrays:
                if len(array.shape) == 3:
                    pieces = [array[k] for k in range(array.shape[0])]
                else:
                    pieces = [array[:, pl.ds(k * 1024, 1024)] for k in range(array.shape[1] // 1024)]
                for piece in pieces:
                    high = piece.astype(BF16)
                    held[slot, 0:64] = high
                    held[slot, 64:128] = (piece - high.astype(F32)).astype(BF16)
                    slot += 1

        hold(row_held, row_in)
        hold(col_held, col_in)
        row_total[...] = jnp.zeros_like(row_total)
        col_total[...] = jnp.zeros_like(col_total)

    def times(values, tile_high, tile_low, contract):
        dims = (((1,), (contract,)), ((), ()))
        both = lax.dot_general(values, tile_high, dims, preferred_element_type=F32)
        low = lax.dot_general(values[:64], tile_low, dims, preferred_element_type=F32)
        return both[:64] + both[64:] + low

    for g in range(GROUP):
        t = step * GROUP + g
        row_lane = pl.ds(pl.multiple_of(index[4, t], BLOCK), BLOCK)
        col_lane = pl.ds(pl.multiple_of(index[5, t], BLOCK), BLOCK)
        mirror = index[6, t].astype(F32)
        high, low = tiles[g, 0], tiles[g, 1]
        direct = times(col_held[index[1, t], :, col_lane], high, low, 1)
        mirrored = times(row_held[index[0, t], :, row_lane], high, low, 0)
        row_total[index[2, t], :, row_lane] += direct
        col_total[index[3, t], :, col_lane] += mirrored * mirror

    @pl.when(step == pl.num_programs(0) - 1)
    def _():
        if flat:
            for total, out in ((row_total, row_out[0]), (col_total, col_out[0])):
                for k in range(total.shape[0]):
                    out[:, pl.ds(k * 1024, 1024)] = total[k]
        else:
            for k in range(2):
                row_out[k][...] = row_total[k * 8 : k * 8 + 8]
            for k in range(4):
                col_out[k][...] = col_total[k * 2 : k * 2 + 2]


def products(index, tiles, row_in, col_in, flat):
    count = tiles.shape[0]
    whole = lambda v: pl.BlockSpec(v.shape, lambda i, *_: (0,) * len(v.shape))
    if flat:
        outs = [jax.ShapeDtypeStruct((64, n * 1024), F32) for n in (16, 8)]
    else:
        outs = [jax.ShapeDtypeStruct((8, 64, 1024), F32)] * 2
        outs += [jax.ShapeDtypeStruct((2, 64, 1024), F32)] * 4
    return pl.pallas_call(
        functools.partial(product_kernel, len(row_in), len(col_in), flat),
        out_shape=tuple(outs),
        grid_spec=pltpu.PrefetchScalarGridSpec(
            num_scalar_prefetch=1,
            grid=(count // GROUP,),
            in_specs=[pl.BlockSpec((GROUP, 2, BLOCK, BLOCK), lambda i, *_: (i, 0, 0, 0))]
            + [whole(v) for v in row_in]
            + [whole(v) for v in col_in],
            out_specs=tuple(whole(v) for v in outs),
            scratch_shapes=[
                pltpu.VMEM((16, 128, 1024), BF16),
                pltpu.VMEM((8, 128, 1024), BF16),
                pltpu.VMEM((16, 64, 1024), F32),
                pltpu.VMEM((8, 64, 1024), F32),
            ],
        ),
        compiler_params=pltpu.CompilerParams(vmem_limit_bytes=60 << 20),
        cost_estimate=pl.CostEstimate(
            flops=count * 12 * 64 * BLOCK * BLOCK,
            bytes_accessed=count * 4 * BLOCK * BLOCK + (12 << 20),
            transcendentals=0,
        ),
        name="slope_products" if flat else "kernel_products",
    )(index, tiles, *row_in, *col_in)


def reduce_parts(row_keep, row_send, cols):
    row_got = flip_core(row_send)
    col_got = [shift_x(cols[s], s) for s in (1, 2, 3)]
    own = [row_keep[2 * s : 2 * s + 2] + row_got[2 * s : 2 * s + 2] for s in range(4)]
    row_recv = [shift_y(own[s], s) for s in (1, 2, 3)]
    col_sum = cols[0] + col_got[0] + col_got[1] + col_got[2]
    row_sum = own[0] + row_recv[0] + row_recv[1] + row_recv[2]
    return row_sum[0] + col_sum[0] + flip_z_lo(row_sum[1]) + flip_z_hi(col_sum[1])


def on_device(
    points, point_order, noise_var, inv_scale, basis_vectors, current, tile_rows, tile_cols
):
    per_device = points.shape[1]
    row_at = lax.axis_index("row")
    col_at = lax.axis_index("col")
    point_total = per_device * 128
    arrangement = point_order[0]
    arranged = jnp.take(points, arrangement, axis=1)
    noise_here = jnp.take(noise_var, arrangement)
    row_blocks = tile_rows[0, 0]
    col_blocks = tile_cols[0, 0]
    row_owner, row_sub = row_blocks // 4, row_blocks % 4
    col_owner, col_sub = col_blocks // 4, col_blocks % 4
    mirror = ((row_at * 16 + row_owner) * 4 + row_sub) != (
        (col_owner * 16 + col_at) * 4 + col_sub
    )
    core_rel = (row_owner ^ col_at) & 1
    zlo_rel = ((row_owner ^ col_at) >> 1) & 1
    y_to = (row_owner // 4 - col_at // 4) & 3
    zhi_rel = (col_owner ^ row_at) & 1
    x_to = (col_owner // 2 - row_at // 2) & 3
    row_from = core_rel * 8 + ((4 - y_to) & 3) * 2 + zlo_rel
    row_to = core_rel * 8 + y_to * 2 + zlo_rel
    col_from = ((4 - x_to) & 3) * 2 + zhi_rel
    col_to = x_to * 2 + zhi_rel

    def table(row_in, col_in, row_out, col_out):
        rows = [row_in, col_in, row_out, col_out, row_sub * BLOCK, col_sub * BLOCK, mirror]
        return jnp.stack([v.astype(jnp.int32) for v in rows])

    pairs = lambda arrays: jnp.concatenate([a[k] for a in arrays for k in range(2)], axis=1)
    col_points = pairs(gather_row_group(arranged))
    row_points = pairs(gather_col_group(arranged))
    kern, slope = make_tiles(
        row_from * 1024 + row_sub * BLOCK,
        col_from * 1024 + col_sub * BLOCK,
        row_points,
        col_points,
        inv_scale[:, None],
    )

    earlier = basis_vectors
    coefficient_rows = []
    gradient_product = current
    for iteration in range(ITERS):
        if iteration == 0:
            row_in = [lax.all_gather(current, "col", axis=1, tiled=True)]
            in_slots = row_owner
        else:
            row_in = gather_col_group(current)
            in_slots = row_from
        col_in = gather_row_group(current)
        parts = products(table(in_slots, col_from, row_to, col_to), kern, row_in, col_in, False)
        image_vec = reduce_parts(parts[0], parts[1], parts[2:]) + noise_here * current
        if iteration == 0:
            row_part, col_part = products(
                table(in_slots, col_from, row_owner, col_owner), slope, row_in, col_in, True
            )
            gradient_product = lax.psum_scatter(
                row_part, "col", scatter_dimension=1, tiled=True
            ) + lax.psum_scatter(col_part, "row", scatter_dimension=1, tiled=True)
        dots = jnp.concatenate(
            [
                jnp.einsum("hpn,pn->hp", earlier, image_vec, precision=HIGHEST),
                jnp.sum(current * image_vec, axis=1)[None],
            ]
        )
        dots = sum_everywhere(dots) / point_total
        alpha_now = dots[-1]
        residual_vec = (
            image_vec
            - alpha_now[:, None] * current
            - jnp.einsum("hp,hpn->pn", dots[:-1], earlier, precision=HIGHEST)
        )
        residual_sq = (
            sum_everywhere(jnp.sum(residual_vec * residual_vec, axis=1)[None])[0] / point_total
        )
        beta_now = jnp.sqrt(residual_sq + EPSILON)
        coefficient_rows += [alpha_now, beta_now]
        if iteration + 1 < ITERS:
            earlier = jnp.concatenate([earlier, current[None]], axis=0)
        current = residual_vec / beta_now[:, None]
    return (current, jnp.stack(coefficient_rows), gradient_product)


def solution(mesh):
    return jax.shard_map(
        on_device,
        mesh=mesh,
        in_specs=(
            P(None, ("row", "col")),
            P(("row", "col"), None),
            P(("row", "col")),
            P(),
            P(None, None, ("row", "col")),
            P(None, ("row", "col")),
            P("row", "col", None),
            P("row", "col", None),
        ),
        out_specs=(P(None, ("row", "col")), P(), P(None, ("row", "col"))),
        check_vma=False,
    )
```

```python
import functools
import math

import jax
import jax.numpy as jnp
from jax import lax
from jax.experimental import pallas as pl
from jax.experimental.pallas import tpu as pltpu
from jax.sharding import PartitionSpec as P


BLOCK = 256
GROUP = 4

ROOT_THREE = math.sqrt(3.0)
SUPPORT = 3.0
EPSILON = 1e-06
F32 = jnp.float32
BF16 = jnp.bfloat16


def shift_y(v, s):
    return lax.ppermute(v, "col", [(i, (i + 4 * s) % 16) for i in range(16)])


def shift_x(v, s):
    return lax.ppermute(v, "row", [(i, (i + 2 * s) % 8) for i in range(8)])


def flip_core(v):
    return lax.ppermute(v, "col", [(i, i ^ 1) for i in range(16)])


def flip_z_lo(v):
    return lax.ppermute(v, "col", [(i, i ^ 2) for i in range(16)])


def flip_z_hi(v):
    return lax.ppermute(v, "row", [(i, i ^ 1) for i in range(8)])


def sum_everywhere(v):
    for axis, size, bits in (("col", 16, (1, 2, 4, 8)), ("row", 8, (1, 2, 4))):
        for bit in bits:
            v = v + lax.ppermute(v, axis, [(i, i ^ bit) for i in range(size)])
    return v


def gather_points(v):
    rows, cols = v[None], v[None]
    for row_bit, col_bit in ((2, 1), (4, 2), (8, 4), (1, None)):
        more = lax.ppermute(rows, "col", [(i, i ^ row_bit) for i in range(16)])
        rows = jnp.concatenate([rows, more])
        if col_bit is not None:
            more = lax.ppermute(cols, "row", [(i, i ^ col_bit) for i in range(8)])
            cols = jnp.concatenate([cols, more])
    return rows, cols


def gather_row_group(v):
    pair = jnp.stack([v, flip_z_hi(v)])
    return [pair] + [shift_x(pair, s) for s in (1, 2, 3)]


def gather_col_group(v):
    pair = jnp.stack([v, flip_z_lo(v)])
    own = [pair] + [shift_y(pair, s) for s in (1, 2, 3)]
    return own + [flip_core(v) for v in own]


def split_three(v):
    high = v.astype(BF16).astype(F32)
    rest = v - high
    middle = rest.astype(BF16).astype(F32)
    return high, middle, rest - middle


def split_two(v):
    scaled = v * 65537.0
    high = scaled - (scaled - v)
    return high, v - high


def tile_kernel(row_at, col_at, row_points, col_points, scale, kern, slope, left, right):
    @pl.when(pl.program_id(0) == 0)
    def _():
        def features(points, is_left):
            scaled = points * scale[...]
            size = scaled.shape[1]
            norm = split_three(jnp.sum(scaled * scaled, axis=0, keepdims=True))
            one = jnp.ones((1, size), F32)
            none = jnp.zeros((2, size), F32)
            if is_left:
                high, middle, low = split_three(scaled)
                parts = [high, high, middle, middle, high, low, *norm, one, one, one]
            else:
                high, middle, low = split_three(-2.0 * scaled)
                parts = [high, middle, high, middle, low, high, one, one, one, *norm]
            parts += [none, jnp.zeros((8, size), F32)]
            return jnp.concatenate(parts, axis=0).astype(BF16)

        width = row_points.shape[2]
        for held, points in ((left, row_points), (right, col_points)):
            for k in range(points.shape[0]):
                held[:, pl.ds(k * width, width)] = features(points[k], held is left)

    base = pl.program_id(0) * GROUP
    for g in range(GROUP):
        row_lane = pl.multiple_of(row_at[base + g], BLOCK)
        col_lane = pl.multiple_of(col_at[base + g], BLOCK)
        dist_sq = lax.dot_general(
            left[:, pl.ds(row_lane, BLOCK)],
            right[:, pl.ds(col_lane, BLOCK)],
            (((0,), (0,)), ((), ())),
            preferred_element_type=F32,
        )
        shifted = jnp.maximum(dist_sq, 0.0) + EPSILON
        radius = shifted * lax.rsqrt(shifted)
        decaying = jnp.exp2(radius * (-ROOT_THREE / math.log(2.0)))
        tapered = jnp.maximum(1.0 - radius * (1.0 / SUPPORT), 0.0)
        common = decaying * (tapered * tapered * tapered)
        weight = tapered * (3.0 + (12.0 / SUPPORT) * radius)
        growing = (1.0 / 3.0) + (ROOT_THREE / 3.0) * radius
        kernel_tile = common * weight * growing
        slope_tile = shifted * common * (weight + (60.0 / (SUPPORT * SUPPORT)) * growing)
        for out, tile in ((kern, kernel_tile), (slope, slope_tile)):
            high, low = split_two(tile)
            out[g, 0] = high.astype(BF16)
            out[g, 1] = low.astype(BF16)


def make_tiles(row_at, col_at, row_points, col_points, scale):
    tiles = row_at.shape[0]
    whole = lambda v: pl.BlockSpec(v.shape, lambda i, *_: (0,) * v.ndim)
    out_spec = pl.BlockSpec((GROUP, 2, BLOCK, BLOCK), lambda i, *_: (i, 0, 0, 0))
    out = jax.ShapeDtypeStruct((tiles, 2, BLOCK, BLOCK), BF16)
    return pl.pallas_call(
        tile_kernel,
        out_shape=(out, out),
        grid_spec=pltpu.PrefetchScalarGridSpec(
            num_scalar_prefetch=2,
            grid=(tiles // GROUP,),
            in_specs=[whole(row_points), whole(col_points), whole(scale)],
            out_specs=(out_spec, out_spec),
            scratch_shapes=[
                pltpu.VMEM((64, row_points.shape[0] * 1024), BF16),
                pltpu.VMEM((64, col_points.shape[0] * 1024), BF16),
            ],
        ),
        compiler_params=pltpu.CompilerParams(vmem_limit_bytes=48 << 20),
        cost_estimate=pl.CostEstimate(
            flops=tiles * 30 * BLOCK * BLOCK,
            bytes_accessed=tiles * 8 * BLOCK * BLOCK,
            transcendentals=tiles * 2 * BLOCK * BLOCK,
        ),
        name="make_tiles",
    )(row_at, col_at, row_points, col_points, scale)


def product_kernel(row_count, col_count, flat, index, tiles, *refs):
    row_in, refs = refs[:row_count], refs[row_count:]
    col_in, refs = refs[:col_count], refs[col_count:]
    outs, refs = refs[: 3 if flat else 6], refs[3 if flat else 6 :]
    tiles_here, row_held, col_held, row_total, col_total, arrived, left = refs

    def fetch(step):
        some = pl.ds(step * GROUP, GROUP)
        return pltpu.make_async_copy(tiles.at[some], tiles_here.at[some], arrived.at[step])

    steps = tiles.shape[0] // GROUP

    @pl.loop(0, steps)
    def _(step):
        fetch(step).start()

    def hold(held, arrays):
        slot = 0
        for array in arrays:
            if len(array.shape) == 3:
                pieces = [array.at[k] for k in range(array.shape[0])]
            else:
                pieces = [array.at[:, pl.ds(k * 1024, 1024)] for k in range(array.shape[1] // 1024)]
            for piece in pieces:
                value = piece[...]
                high = value.astype(BF16)
                held[slot, 0:64] = high
                held[slot, 64:128] = (value - high.astype(F32)).astype(BF16)
                slot += 1

    hold(row_held, row_in)
    hold(col_held, col_in)
    row_total[...] = jnp.zeros_like(row_total)
    col_total[...] = jnp.zeros_like(col_total)

    def times(values, tile_high, tile_low, contract):
        dims = (((1,), (contract,)), ((), ()))
        both = lax.dot_general(values, tile_high, dims, preferred_element_type=F32)
        low = lax.dot_general(values[:64], tile_low, dims, preferred_element_type=F32)
        return both[:64] + both[64:] + low

    @pl.loop(0, steps)
    def _(step):
        fetch(step).wait()
        for g in range(GROUP):
            t = step * GROUP + g
            row_lane = pl.ds(pl.multiple_of(index[4, t], BLOCK), BLOCK)
            col_lane = pl.ds(pl.multiple_of(index[5, t], BLOCK), BLOCK)
            mirror = index[6, t].astype(F32)
            high, low = tiles_here[t, 0], tiles_here[t, 1]
            direct = times(col_held[index[1, t], :, col_lane], high, low, 1)
            mirrored = times(row_held[index[0, t], :, row_lane], high, low, 0)
            row_total[index[2, t], :, row_lane] += direct
            col_total[index[3, t], :, col_lane] += mirrored * mirror

    if flat:
        slots = [row_total.at[k] for k in range(16)] + [col_total.at[k] for k in range(8)]
        places = [out.at[:, pl.ds(k * 1024, 1024)] for out in outs for k in range(8)]
    else:
        slots = [row_total.at[pl.ds(k * 8, 8)] for k in (0, 1)]
        slots += [col_total.at[pl.ds(k * 2, 2)] for k in range(4)]
        places = outs
    copies = [
        pltpu.make_async_copy(slot, place, left.at[k])
        for k, (slot, place) in enumerate(zip(slots, places))
    ]
    for copy in copies:
        copy.start()
    for copy in copies:
        copy.wait()


def products(index, tiles, row_in, col_in, flat):
    count = tiles.shape[0]
    here = pl.BlockSpec(memory_space=pltpu.VMEM)
    if flat:
        outs = [jax.ShapeDtypeStruct((64, 8 * 1024), F32)] * 3
    else:
        outs = [jax.ShapeDtypeStruct((8, 64, 1024), F32)] * 2
        outs += [jax.ShapeDtypeStruct((2, 64, 1024), F32)] * 4
    return pl.pallas_call(
        functools.partial(product_kernel, len(row_in), len(col_in), flat),
        out_shape=tuple(outs),
        in_specs=[pl.BlockSpec(memory_space=pltpu.SMEM), pl.BlockSpec(memory_space=pltpu.HBM)]
        + [here] * (len(row_in) + len(col_in)),
        out_specs=tuple(pl.BlockSpec(memory_space=pltpu.HBM) for _ in outs),
        scratch_shapes=[
            pltpu.VMEM(tiles.shape, BF16),
            pltpu.VMEM((16, 128, 1024), BF16),
            pltpu.VMEM((8, 128, 1024), BF16),
            pltpu.VMEM((16, 64, 1024), F32),
            pltpu.VMEM((8, 64, 1024), F32),
            pltpu.SemaphoreType.DMA((count // GROUP,)),
            pltpu.SemaphoreType.DMA((24,)),
        ],
        compiler_params=pltpu.CompilerParams(vmem_limit_bytes=60_200_000),
        cost_estimate=pl.CostEstimate(
            flops=count * 12 * 64 * BLOCK * BLOCK,
            bytes_accessed=count * 4 * BLOCK * BLOCK + (12 << 20),
            transcendentals=0,
        ),
        name="slope_products" if flat else "kernel_products",
    )(index, tiles, *row_in, *col_in)


def column_sums(pairs, columns):
    lane = lax.broadcasted_iota(jnp.int32, (8, columns), 1)
    held = jnp.zeros((8, columns), F32)
    for k, (a, b) in enumerate(pairs):
        held = jnp.where(lane == k, jnp.sum(a * b, axis=1, keepdims=True), held)
    return held


def row_blocks_of(rows):
    return lambda body: pl.loop(0, rows // 8)(
        lambda step: body(pl.ds(pl.multiple_of(step * 8, 8), 8))
    )


def vectors_at(earlier, extra, at):
    return [earlier[h, at] for h in range(earlier.shape[0])] + [v[at] for v in extra]


def dots_kernel(piece_count, extra_count, earlier, noise, *refs):
    pieces, refs = refs[:piece_count], refs[piece_count:]
    extra, (image_out, dots_out, held) = refs[:extra_count], refs[extra_count:]
    held[...] = jnp.zeros_like(held)

    @row_blocks_of(image_out.shape[0])
    def _(at):
        image = noise[...] * extra[-1][at]
        for piece in pieces:
            if len(piece.shape) == 3:
                image = image + piece[0, at]
            else:
                image = image + piece[at]
        image_out[at] = image
        vectors = vectors_at(earlier, extra, at) + [image]
        held[at] = column_sums([(v, image) for v in vectors], 128)

    dots_out[...] = held[...].T[: dots_out.shape[0]]


def image_dots(earlier, noise, pieces, extra):
    rows, lanes = extra[-1].shape
    return pl.pallas_call(
        functools.partial(dots_kernel, len(pieces), len(extra)),
        out_shape=(
            jax.ShapeDtypeStruct((rows, lanes), F32),
            jax.ShapeDtypeStruct((24, 128), F32),
        ),
        scratch_shapes=[pltpu.VMEM((128, 128), F32)],
        compiler_params=pltpu.CompilerParams(vmem_limit_bytes=2 << 20),
        cost_estimate=pl.CostEstimate(
            flops=rows * lanes * 60, bytes_accessed=rows * lanes * 4 * 30, transcendentals=0
        ),
        name="image_dots",
    )(earlier, noise, *pieces, *extra)


def gram_kernel(earlier, first, out, held):
    held[...] = jnp.zeros_like(held)

    @row_blocks_of(first.shape[0])
    def _(at):
        vectors = vectors_at(earlier, [first], at)
        count = len(vectors)
        pairs = [(vectors[i], vectors[i + d]) for d in range(count) for i in range(count - d)]
        held[at, 0:128] = column_sums(pairs[:128], 128)
        held[at, 128:256] = column_sums(pairs[128:], 128)

    out[0:128] = held[:, 0:128].T
    out[128:160] = held[:, 128:256].T[:32]


def gram_sums(earlier, first):
    rows, lanes = first.shape
    return pl.pallas_call(
        gram_kernel,
        out_shape=jax.ShapeDtypeStruct((160, 128), F32),
        scratch_shapes=[pltpu.VMEM((128, 256), F32)],
        compiler_params=pltpu.CompilerParams(vmem_limit_bytes=2 << 20),
        cost_estimate=pl.CostEstimate(
            flops=rows * lanes * 400, bytes_accessed=rows * lanes * 4 * 18, transcendentals=0
        ),
        name="gram_sums",
    )(earlier, first)


def turned(values):
    rows = values.shape[0]
    return jnp.concatenate([values, jnp.zeros((128 - rows, 128), F32)], axis=0).T


def combine(columns, image, vectors):
    total = columns[:, 0:1] * image
    for k, v in enumerate(vectors):
        total = total - columns[:, k + 1 : k + 2] * v
    return total


def first_rest_kernel(total, sums, image, earlier, first, rest, held):
    means = sums[0:17] * (1.0 / total)
    held[...] = turned(jnp.concatenate([jnp.ones((1, 128), F32), means], axis=0))

    @row_blocks_of(rest.shape[0])
    def _(at):
        rest[at] = combine(held[at], image[at], vectors_at(earlier, [first], at))


def last_rest_kernel(
    total, sums, next_sums, gram, image, earlier, first, second, out, coefficients, held
):
    count = 17
    means = sums[...] * (1.0 / total)
    along = means[0:count]
    turned_along = jnp.zeros((count, 128), F32)
    at = 0
    diagonals = []
    for d in range(count):
        size = count - d
        diagonal = gram[at : at + size] * (1.0 / total)
        diagonals.append(diagonal)
        part = diagonal * along[d:]
        if d:
            other = diagonal * along[:size]
            blank = jnp.zeros((d, 128), F32)
            part = jnp.concatenate([part, blank], axis=0) + jnp.concatenate([blank, other], axis=0)
        turned_along = turned_along + part
        at += size
    rest_means = along - turned_along
    column = lambda v: jnp.sum(v, axis=0, keepdims=True)
    norm = means[17:18] - 2.0 * column(along * along) + column(along * turned_along)
    norm = jnp.maximum(norm, 0.0)
    norm_sq = norm + EPSILON
    scale = 1.0 / jnp.sqrt(norm_sq)

    next_means = next_sums[...] * (1.0 / total)
    next_along = next_means[0:count] * scale
    alpha = next_means[17:18] * (scale * scale)
    beside = alpha * scale
    rest_sq = (
        next_means[18:19] * (scale * scale)
        - 2.0 * (column(next_along * next_along) + alpha * alpha)
        + 2.0 * beside * column(next_along * rest_means)
        + beside * beside * norm
    )
    for d in range(count):
        part = column(next_along[: count - d] * next_along[d:] * diagonals[d])
        rest_sq = rest_sq + (1.0 if d == 0 else 2.0) * part
    beta = jnp.sqrt(jnp.maximum(rest_sq, 0.0) + EPSILON)
    held[...] = turned(jnp.concatenate([scale, next_along, beside], axis=0) / beta)
    coefficients[...] = jnp.concatenate(
        [along[16:17], jnp.sqrt(norm_sq), alpha, beta, jnp.zeros((4, 128), F32)], axis=0
    )

    @row_blocks_of(out.shape[0])
    def _(at):
        out[at] = combine(held[at], image[at], vectors_at(earlier, [first, second], at))


def rest_call(kernel, total, smalls, image, earlier, extra, with_coefficients):
    rows, lanes = image.shape
    out_shape = [jax.ShapeDtypeStruct((rows, lanes), F32)]
    if with_coefficients:
        out_shape.append(jax.ShapeDtypeStruct((8, 128), F32))
    return pl.pallas_call(
        functools.partial(kernel, float(total)),
        out_shape=tuple(out_shape),
        scratch_shapes=[pltpu.VMEM((128, 128), F32)],
        compiler_params=pltpu.CompilerParams(vmem_limit_bytes=2 << 20),
        cost_estimate=pl.CostEstimate(
            flops=rows * lanes * 40, bytes_accessed=rows * lanes * 4 * 20, transcendentals=0
        ),
    )(*smalls, image, earlier, *extra)


def reduce_parts(parts):
    row_keep, row_send, cols = parts[0], parts[1], parts[2:]
    row_got = flip_core(row_send)
    col_got = []
    for s in (2, 1, 3):
        col_got.append(shift_x(cols[s], s))
    own = [row_keep[2 * s : 2 * s + 2] + row_got[2 * s : 2 * s + 2] for s in range(4)]
    row_got = []
    for s in (2, 1, 3):
        row_got.append(shift_y(own[s], s))
    col_sum = cols[0] + col_got[0] + col_got[1] + col_got[2]
    row_sum = own[0] + row_got[0] + row_got[1] + row_got[2]
    return [col_sum, row_sum, flip_z_hi(col_sum[1]), flip_z_lo(row_sum[1])]


def on_device(
    points, point_order, noise_var, inv_scale, basis_vectors, current, tile_rows, tile_cols
):
    per_device = points.shape[1]
    row_at = lax.axis_index("row")
    col_at = lax.axis_index("col")
    point_total = per_device * 128
    arrangement = point_order[0]
    arranged = jnp.take(points, arrangement, axis=1)
    noise_here = jnp.take(noise_var, arrangement)
    row_blocks = tile_rows[0, 0]
    col_blocks = tile_cols[0, 0]
    row_owner, row_sub = row_blocks // 4, row_blocks % 4
    col_owner, col_sub = col_blocks // 4, col_blocks % 4
    mirror = ((row_at * 16 + row_owner) * 4 + row_sub) != (
        (col_owner * 16 + col_at) * 4 + col_sub
    )
    core_rel = (row_owner ^ col_at) & 1
    zlo_rel = ((row_owner ^ col_at) >> 1) & 1
    y_to = (row_owner // 4 - col_at // 4) & 3
    zhi_rel = (col_owner ^ row_at) & 1
    x_to = (col_owner // 2 - row_at // 2) & 3
    row_from = core_rel * 8 + ((4 - y_to) & 3) * 2 + zlo_rel
    row_to = core_rel * 8 + y_to * 2 + zlo_rel
    col_from = ((4 - x_to) & 3) * 2 + zhi_rel
    col_to = x_to * 2 + zhi_rel

    def table(row_in, col_in, row_out, col_out):
        rows = [row_in, col_in, row_out, col_out, row_sub * BLOCK, col_sub * BLOCK, mirror]
        return jnp.stack([v.astype(jnp.int32) for v in rows])

    row_points, col_points = gather_points(arranged)
    row_xor, col_xor = row_owner ^ col_at, col_owner ^ row_at
    kern, slope = make_tiles(
        ((row_xor & 1) * 8 + (row_xor >> 1)) * 1024 + row_sub * BLOCK,
        col_xor * 1024 + col_sub * BLOCK,
        row_points,
        col_points,
        inv_scale[:, None],
    )

    noise = noise_here[None]
    row_in = [lax.all_gather(current, "col", axis=1, tiled=True)]
    kern, current_later = lax.optimization_barrier((kern, current))
    first_table = table(row_owner, col_from, row_to, col_to)
    gram, first_table = lax.optimization_barrier(
        (gram_sums(basis_vectors, current_later), first_table)
    )
    gram = lax.psum(gram, ("row", "col"))
    col_in = gather_row_group(current)
    parts = products(first_table, kern, row_in, col_in, False)
    pieces = reduce_parts(parts)
    slope_to = core_rel * 8 + (row_owner >> 1)
    row_keep, row_send, col_part = products(
        table(row_owner, col_from, slope_to, col_owner), slope, row_in, col_in, True
    )
    col_sum = lax.psum_scatter(col_part, "row", scatter_dimension=1, tiled=True)
    row_part = row_keep + flip_core(row_send)
    row_sum = lax.psum_scatter(
        row_part,
        "col",
        scatter_dimension=1,
        tiled=True,
        axis_index_groups=[[i * 2 + core for i in range(8)] for core in range(2)],
    )
    gradient_product = row_sum + col_sum
    image, sums = image_dots(basis_vectors, noise, pieces, [current])
    sums = sum_everywhere(sums)
    (rest,) = rest_call(
        first_rest_kernel, point_total, [sums], image, basis_vectors, [current], False
    )

    row_in = gather_col_group(rest)
    col_in = gather_row_group(rest)
    parts = products(table(row_from, col_from, row_to, col_to), kern, row_in, col_in, False)
    pieces = reduce_parts(parts)
    image, next_sums = image_dots(basis_vectors, noise, pieces, [current, rest])
    next_sums = sum_everywhere(next_sums)
    lanczos_next, rows = rest_call(
        last_rest_kernel,
        point_total,
        [sums, next_sums, gram],
        image,
        basis_vectors,
        [current, rest],
        True,
    )
    return (lanczos_next, rows[:4, :64], gradient_product)


def solution(mesh):
    return jax.shard_map(
        on_device,
        mesh=mesh,
        in_specs=(
            P(None, ("row", "col")),
            P(("row", "col"), None),
            P(("row", "col")),
            P(),
            P(None, None, ("row", "col")),
            P(None, ("row", "col")),
            P("row", "col", None),
            P("row", "col", None),
        ),
        out_specs=(P(None, ("row", "col")), P(), P(None, ("row", "col"))),
        check_vma=False,
    )
```

```python
import functools
import math

import jax
import jax.numpy as jnp
from jax import lax
from jax.experimental import pallas as pl
from jax.experimental.pallas import tpu as pltpu
from jax.sharding import PartitionSpec as P


BLOCK = 256
GROUP = 4

ROOT_THREE = math.sqrt(3.0)
SUPPORT = 3.0
EPSILON = 1e-06
F32 = jnp.float32
BF16 = jnp.bfloat16


def shift_y(v, s):
    return lax.ppermute(v, "col", [(i, (i + 4 * s) % 16) for i in range(16)])


def shift_x(v, s):
    return lax.ppermute(v, "row", [(i, (i + 2 * s) % 8) for i in range(8)])


def flip_core(v):
    return lax.ppermute(v, "col", [(i, i ^ 1) for i in range(16)])


def flip_z_lo(v):
    return lax.ppermute(v, "col", [(i, i ^ 2) for i in range(16)])


def flip_z_hi(v):
    return lax.ppermute(v, "row", [(i, i ^ 1) for i in range(8)])


def sum_everywhere(v):
    for axis, size, bits in (("col", 16, (1, 2, 4, 8)), ("row", 8, (1, 2, 4))):
        for bit in bits:
            v = v + lax.ppermute(v, axis, [(i, i ^ bit) for i in range(size)])
    return v


def gather_points(v):
    rows, cols = v[None], v[None]
    for row_bit, col_bit in ((2, 1), (4, 2), (8, 4), (1, None)):
        more = lax.ppermute(rows, "col", [(i, i ^ row_bit) for i in range(16)])
        rows = jnp.concatenate([rows, more])
        if col_bit is not None:
            more = lax.ppermute(cols, "row", [(i, i ^ col_bit) for i in range(8)])
            cols = jnp.concatenate([cols, more])
    return rows, cols


def gather_row_group(v):
    pair = jnp.stack([v, flip_z_hi(v)])
    gathered = [pair]
    for s in (1, 2, 3):
        gathered.append(shift_x(pair, s))
    return gathered


def gather_col_group(v):
    pair = jnp.stack([v, flip_z_lo(v)])
    own = [pair] + [shift_y(pair, s) for s in (1, 2, 3)]
    return own + [flip_core(v) for v in own]


def split_three(v):
    high = v.astype(BF16).astype(F32)
    rest = v - high
    middle = rest.astype(BF16).astype(F32)
    return high, middle, rest - middle


def split_two(v):
    scaled = v * 65537.0
    high = scaled - (scaled - v)
    return high, v - high


def features(points, is_left):
    size = points.shape[1]
    norm = split_three(jnp.sum(points * points, axis=0, keepdims=True))
    one = jnp.ones((1, size), F32)
    if is_left:
        high, middle, low = split_three(points)
        parts = [high, high, middle, middle, high, low, *norm, one, one, one]
    else:
        high, middle, low = split_three(-2.0 * points)
        parts = [high, middle, high, middle, low, high, one, one, one, *norm]
    parts += [jnp.zeros((10, size), F32)]
    return jnp.concatenate(parts, axis=0).astype(BF16)


def tile_of(dist_sq, is_slope):
    shifted = jnp.maximum(dist_sq, 0.0) + EPSILON
    radius = shifted * lax.rsqrt(shifted)
    decaying = jnp.exp2(radius * (-ROOT_THREE / math.log(2.0)))
    tapered = jnp.maximum(1.0 - radius * (1.0 / SUPPORT), 0.0)
    common = decaying * (tapered * tapered * tapered)
    weight = tapered * (3.0 + (12.0 / SUPPORT) * radius)
    growing = (1.0 / 3.0) + (ROOT_THREE / 3.0) * radius
    if is_slope:
        return shifted * common * (weight + (60.0 / (SUPPORT * SUPPORT)) * growing)
    return common * weight * growing


def product_kernel(row_count, col_count, kind, index, *refs):
    if kind == "again":
        tiles, refs = refs[0], refs[1:]
    else:
        (row_points, col_points, scale), refs = refs[:3], refs[3:]
    row_in, refs = refs[:row_count], refs[row_count:]
    col_in, refs = refs[:col_count], refs[col_count:]
    if kind == "kernel":
        tiles, refs = refs[0], refs[1:]
    outs, refs = refs[: 3 if kind == "slope" else 6], refs[3 if kind == "slope" else 6 :]
    here, row_held, col_held, row_total, col_total, moved, left_at = refs[:7]
    steps = index.shape[1] // GROUP

    def move(step):
        some = pl.ds(step * GROUP, GROUP)
        if kind == "again":
            return pltpu.make_async_copy(tiles.at[some], here.at[some], moved.at[step])
        return pltpu.make_async_copy(here.at[some], tiles.at[some], moved.at[step])

    if kind == "again":

        @pl.loop(0, steps)
        def _(step):
            move(step).start()

    else:
        left, right = refs[7:]
        for held, points in ((left, row_points), (right, col_points)):
            for k in range(points.shape[0]):
                held[:, pl.ds(k * 1024, 1024)] = features(points[k] * scale[...], held is left)

    def hold(held, arrays):
        slot = 0
        for array in arrays:
            if len(array.shape) == 3:
                pieces = [array.at[k] for k in range(array.shape[0])]
            else:
                pieces = [array.at[:, pl.ds(k * 1024, 1024)] for k in range(array.shape[1] // 1024)]
            for piece in pieces:
                value = piece[...]
                high = value.astype(BF16)
                held[slot, 0:64] = high
                held[slot, 64:128] = (value - high.astype(F32)).astype(BF16)
                slot += 1

    hold(row_held, row_in)
    hold(col_held, col_in)
    row_total[...] = jnp.zeros_like(row_total)
    col_total[...] = jnp.zeros_like(col_total)

    def times(values, tile_high, tile_low, contract):
        dims = (((1,), (contract,)), ((), ()))
        both = lax.dot_general(values, tile_high, dims, preferred_element_type=F32)
        low = lax.dot_general(values[:64], tile_low, dims, preferred_element_type=F32)
        return both[:64] + both[64:] + low

    @pl.loop(0, steps)
    def _(step):
        if kind == "again":
            move(step).wait()
        for g in range(GROUP):
            t = step * GROUP + g
            at = g if kind == "slope" else t
            if kind != "again":
                row_point = pl.ds(pl.multiple_of(index[7, t], BLOCK), BLOCK)
                col_point = pl.ds(pl.multiple_of(index[8, t], BLOCK), BLOCK)
                dist_sq = lax.dot_general(
                    left[:, row_point],
                    right[:, col_point],
                    (((0,), (0,)), ((), ())),
                    preferred_element_type=F32,
                )
                high, low = split_two(tile_of(dist_sq, kind == "slope"))
                here[at, 0] = high.astype(BF16)
                here[at, 1] = low.astype(BF16)
            row_lane = pl.ds(pl.multiple_of(index[4, t], BLOCK), BLOCK)
            col_lane = pl.ds(pl.multiple_of(index[5, t], BLOCK), BLOCK)
            mirror = index[6, t].astype(F32)
            high, low = here[at, 0], here[at, 1]
            direct = times(col_held[index[1, t], :, col_lane], high, low, 1)
            mirrored = times(row_held[index[0, t], :, row_lane], high, low, 0)
            row_total[index[2, t], :, row_lane] += direct
            col_total[index[3, t], :, col_lane] += mirrored * mirror
        if kind == "kernel":
            move(step).start()

    if kind == "slope":
        slots = [row_total.at[k] for k in range(16)] + [col_total.at[k] for k in range(8)]
        places = [out.at[:, pl.ds(k * 1024, 1024)] for out in outs for k in range(8)]
    else:
        slots = [row_total.at[pl.ds(k * 8, 8)] for k in (1, 0)]
        slots += [col_total.at[pl.ds(k * 2, 2)] for k in range(4)]
        places = outs
    copies = [
        pltpu.make_async_copy(slot, place, left_at.at[k])
        for k, (slot, place) in enumerate(zip(slots, places))
    ]
    for copy in copies:
        copy.start()
    for copy in copies:
        copy.wait()
    if kind == "kernel":

        @pl.loop(0, steps)
        def _(step):
            move(step).wait()


def products(kind, index, sources, row_in, col_in):
    count = index.shape[1]
    tiles = jax.ShapeDtypeStruct((count, 2, BLOCK, BLOCK), BF16)
    near, far = pl.BlockSpec(memory_space=pltpu.VMEM), pl.BlockSpec(memory_space=pltpu.HBM)
    if kind == "slope":
        outs = [jax.ShapeDtypeStruct((64, 8 * 1024), F32)] * 3
    else:
        outs = [jax.ShapeDtypeStruct((8, 64, 1024), F32)] * 2
        outs += [jax.ShapeDtypeStruct((2, 64, 1024), F32)] * 4
    if kind == "kernel":
        outs = [tiles] + outs
    scratch = [
        pltpu.VMEM((GROUP if kind == "slope" else count, 2, BLOCK, BLOCK), BF16),
        pltpu.VMEM((16, 128, 1024), BF16),
        pltpu.VMEM((8, 128, 1024), BF16),
        pltpu.VMEM((16, 64, 1024), F32),
        pltpu.VMEM((8, 64, 1024), F32),
        pltpu.SemaphoreType.DMA((count // GROUP,)),
        pltpu.SemaphoreType.DMA((24,)),
    ]
    if kind != "again":
        scratch += [pltpu.VMEM((64, 16 * 1024), BF16), pltpu.VMEM((64, 8 * 1024), BF16)]
    return pl.pallas_call(
        functools.partial(product_kernel, len(row_in), len(col_in), kind),
        out_shape=tuple(outs),
        in_specs=[pl.BlockSpec(memory_space=pltpu.SMEM)]
        + [far if kind == "again" else near] * len(sources)
        + [near] * (len(row_in) + len(col_in)),
        out_specs=tuple(far for _ in outs),
        scratch_shapes=scratch,
        compiler_params=pltpu.CompilerParams(vmem_limit_bytes=59_000_000),
        cost_estimate=pl.CostEstimate(
            flops=count * 12 * 64 * BLOCK * BLOCK,
            bytes_accessed=count * 4 * BLOCK * BLOCK + (12 << 20),
            transcendentals=0,
        ),
    )(index, *sources, *row_in, *col_in)


def column_sums(pairs, columns):
    lane = lax.broadcasted_iota(jnp.int32, (8, columns), 1)
    held = jnp.zeros((8, columns), F32)
    for k, (a, b) in enumerate(pairs):
        held = jnp.where(lane == k, jnp.sum(a * b, axis=1, keepdims=True), held)
    return held


def row_blocks_of(rows):
    return lambda body: pl.loop(0, rows // 8)(
        lambda step: body(pl.ds(pl.multiple_of(step * 8, 8), 8))
    )


def vectors_at(earlier, extra, at):
    return [earlier[h, at] for h in range(earlier.shape[0])] + [v[at] for v in extra]


def dots_kernel(piece_count, extra_count, earlier, noise, *refs):
    pieces, refs = refs[:piece_count], refs[piece_count:]
    extra, (image_out, dots_out, held) = refs[:extra_count], refs[extra_count:]
    held[...] = jnp.zeros_like(held)

    @row_blocks_of(image_out.shape[0])
    def _(at):
        image = noise[...] * extra[-1][at]
        for piece in pieces:
            if len(piece.shape) == 3:
                image = image + piece[0, at]
            else:
                image = image + piece[at]
        image_out[at] = image
        vectors = vectors_at(earlier, extra, at) + [image]
        held[at] = column_sums([(v, image) for v in vectors], 128)

    dots_out[...] = held[...].T[: dots_out.shape[0]]


def image_dots(earlier, noise, pieces, extra):
    rows, lanes = extra[-1].shape
    return pl.pallas_call(
        functools.partial(dots_kernel, len(pieces), len(extra)),
        out_shape=(
            jax.ShapeDtypeStruct((rows, lanes), F32),
            jax.ShapeDtypeStruct((24, 128), F32),
        ),
        scratch_shapes=[pltpu.VMEM((128, 128), F32)],
        compiler_params=pltpu.CompilerParams(vmem_limit_bytes=2 << 20),
        cost_estimate=pl.CostEstimate(
            flops=rows * lanes * 60, bytes_accessed=rows * lanes * 4 * 30, transcendentals=0
        ),
        name="image_dots",
    )(earlier, noise, *pieces, *extra)


def gram_kernel(earlier, first, out, held):
    held[...] = jnp.zeros_like(held)

    @row_blocks_of(first.shape[0])
    def _(at):
        vectors = vectors_at(earlier, [first], at)
        count = len(vectors)
        pairs = [(vectors[i], vectors[i + d]) for d in range(count) for i in range(count - d)]
        held[at, 0:128] = column_sums(pairs[:128], 128)
        held[at, 128:256] = column_sums(pairs[128:], 128)

    out[0:128] = held[:, 0:128].T
    out[128:160] = held[:, 128:256].T[:32]


def gram_sums(earlier, first):
    rows, lanes = first.shape
    return pl.pallas_call(
        gram_kernel,
        out_shape=jax.ShapeDtypeStruct((160, 128), F32),
        scratch_shapes=[pltpu.VMEM((128, 256), F32)],
        compiler_params=pltpu.CompilerParams(vmem_limit_bytes=2 << 20),
        cost_estimate=pl.CostEstimate(
            flops=rows * lanes * 400, bytes_accessed=rows * lanes * 4 * 18, transcendentals=0
        ),
        name="gram_sums",
    )(earlier, first)


def turned(values):
    rows = values.shape[0]
    return jnp.concatenate([values, jnp.zeros((128 - rows, 128), F32)], axis=0).T


def combine(columns, image, vectors):
    total = columns[:, 0:1] * image
    for k, v in enumerate(vectors):
        total = total - columns[:, k + 1 : k + 2] * v
    return total


def first_rest_kernel(total, sums, image, earlier, first, rest, held):
    means = sums[0:17] * (1.0 / total)
    held[...] = turned(jnp.concatenate([jnp.ones((1, 128), F32), means], axis=0))

    @row_blocks_of(rest.shape[0])
    def _(at):
        rest[at] = combine(held[at], image[at], vectors_at(earlier, [first], at))


def last_rest_kernel(
    total, sums, next_sums, gram, image, earlier, first, second, out, coefficients, held
):
    count = 17
    means = sums[...] * (1.0 / total)
    along = means[0:count]
    turned_along = jnp.zeros((count, 128), F32)
    at = 0
    diagonals = []
    for d in range(count):
        size = count - d
        diagonal = gram[at : at + size] * (1.0 / total)
        diagonals.append(diagonal)
        part = diagonal * along[d:]
        if d:
            other = diagonal * along[:size]
            blank = jnp.zeros((d, 128), F32)
            part = jnp.concatenate([part, blank], axis=0) + jnp.concatenate([blank, other], axis=0)
        turned_along = turned_along + part
        at += size
    rest_means = along - turned_along
    column = lambda v: jnp.sum(v, axis=0, keepdims=True)
    norm = means[17:18] - 2.0 * column(along * along) + column(along * turned_along)
    norm = jnp.maximum(norm, 0.0)
    norm_sq = norm + EPSILON
    scale = 1.0 / jnp.sqrt(norm_sq)

    next_means = next_sums[...] * (1.0 / total)
    next_along = next_means[0:count] * scale
    alpha = next_means[17:18] * (scale * scale)
    beside = alpha * scale
    rest_sq = (
        next_means[18:19] * (scale * scale)
        - 2.0 * (column(next_along * next_along) + alpha * alpha)
        + 2.0 * beside * column(next_along * rest_means)
        + beside * beside * norm
    )
    for d in range(count):
        part = column(next_along[: count - d] * next_along[d:] * diagonals[d])
        rest_sq = rest_sq + (1.0 if d == 0 else 2.0) * part
    beta = jnp.sqrt(jnp.maximum(rest_sq, 0.0) + EPSILON)
    held[...] = turned(jnp.concatenate([scale, next_along, beside], axis=0) / beta)
    coefficients[...] = jnp.concatenate(
        [along[16:17], jnp.sqrt(norm_sq), alpha, beta, jnp.zeros((4, 128), F32)], axis=0
    )

    @row_blocks_of(out.shape[0])
    def _(at):
        out[at] = combine(held[at], image[at], vectors_at(earlier, [first, second], at))


def rest_call(kernel, total, smalls, image, earlier, extra, with_coefficients):
    rows, lanes = image.shape
    out_shape = [jax.ShapeDtypeStruct((rows, lanes), F32)]
    if with_coefficients:
        out_shape.append(jax.ShapeDtypeStruct((8, 128), F32))
    return pl.pallas_call(
        functools.partial(kernel, float(total)),
        out_shape=tuple(out_shape),
        scratch_shapes=[pltpu.VMEM((128, 128), F32)],
        compiler_params=pltpu.CompilerParams(vmem_limit_bytes=2 << 20),
        cost_estimate=pl.CostEstimate(
            flops=rows * lanes * 40, bytes_accessed=rows * lanes * 4 * 20, transcendentals=0
        ),
    )(*smalls, image, earlier, *extra)


def reduce_parts(parts):
    row_send, row_keep, cols = parts[0], parts[1], parts[2:]
    row_got = flip_core(row_send)
    col_got = []
    for s in (2, 1, 3):
        col_got.append(shift_x(cols[s], s))
    own = [row_keep[2 * s : 2 * s + 2] + row_got[2 * s : 2 * s + 2] for s in range(4)]
    row_got = []
    for s in (2, 1, 3):
        row_got.append(shift_y(own[s], s))
    col_sum = cols[0] + col_got[0] + col_got[1] + col_got[2]
    row_sum = own[0] + row_got[0] + row_got[1] + row_got[2]
    return [col_sum, row_sum, flip_z_hi(col_sum[1]), flip_z_lo(row_sum[1])]


def on_device(
    points, point_order, noise_var, inv_scale, basis_vectors, current, tile_rows, tile_cols
):
    per_device = points.shape[1]
    row_at = lax.axis_index("row")
    col_at = lax.axis_index("col")
    point_total = per_device * 128
    arrangement = point_order[0]
    arranged = jnp.take(points, arrangement, axis=1)
    noise_here = jnp.take(noise_var, arrangement)
    row_blocks = tile_rows[0, 0]
    col_blocks = tile_cols[0, 0]
    row_owner, row_sub = row_blocks // 4, row_blocks % 4
    col_owner, col_sub = col_blocks // 4, col_blocks % 4
    mirror = ((row_at * 16 + row_owner) * 4 + row_sub) != (
        (col_owner * 16 + col_at) * 4 + col_sub
    )
    core_rel = (row_owner ^ col_at) & 1
    zlo_rel = ((row_owner ^ col_at) >> 1) & 1
    y_to = (row_owner // 4 - col_at // 4) & 3
    zhi_rel = (col_owner ^ row_at) & 1
    x_to = (col_owner // 2 - row_at // 2) & 3
    row_from = core_rel * 8 + ((4 - y_to) & 3) * 2 + zlo_rel
    row_to = core_rel * 8 + y_to * 2 + zlo_rel
    col_from = ((4 - x_to) & 3) * 2 + zhi_rel
    col_to = x_to * 2 + zhi_rel

    row_points, col_points = gather_points(arranged)
    row_xor, col_xor = row_owner ^ col_at, col_owner ^ row_at
    row_point = ((row_xor & 1) * 8 + (row_xor >> 1)) * 1024 + row_sub * BLOCK
    col_point = col_xor * 1024 + col_sub * BLOCK

    def table(row_in, col_in, row_out, col_out):
        rows = [row_in, col_in, row_out, col_out, row_sub * BLOCK, col_sub * BLOCK, mirror]
        return jnp.stack([v.astype(jnp.int32) for v in rows + [row_point, col_point]])

    noise = noise_here[None]
    row_in = [lax.all_gather(current, "col", axis=1, tiled=True)]
    col_in = gather_row_group(current)
    gram = gram_sums(basis_vectors, current)
    gram = lax.psum(gram, ("row", "col"))
    sources = [row_points, col_points, inv_scale[:, None]]
    kern, *parts = products(
        "kernel", table(row_owner, col_from, row_to, col_to), sources, row_in, col_in
    )
    pieces = reduce_parts(parts)
    slope_to = core_rel * 8 + (row_owner >> 1)
    row_keep, row_send, col_part = products(
        "slope", table(row_owner, col_from, slope_to, col_owner), sources, row_in, col_in
    )
    col_sum = lax.psum_scatter(col_part, "row", scatter_dimension=1, tiled=True)
    row_part = row_keep + flip_core(row_send)
    row_sum = lax.psum_scatter(
        row_part,
        "col",
        scatter_dimension=1,
        tiled=True,
        axis_index_groups=[[i * 2 + core for i in range(8)] for core in range(2)],
    )
    gradient_product = row_sum + col_sum
    image, sums = image_dots(basis_vectors, noise, pieces, [current])
    sums = sum_everywhere(sums)
    (rest,) = rest_call(
        first_rest_kernel, point_total, [sums], image, basis_vectors, [current], False
    )

    row_in = gather_col_group(rest)
    col_in = gather_row_group(rest)
    parts = products("again", table(row_from, col_from, row_to, col_to), [kern], row_in, col_in)
    pieces = reduce_parts(parts)
    image, next_sums = image_dots(basis_vectors, noise, pieces, [current, rest])
    next_sums = sum_everywhere(next_sums)
    lanczos_next, rows = rest_call(
        last_rest_kernel,
        point_total,
        [sums, next_sums, gram],
        image,
        basis_vectors,
        [current, rest],
        True,
    )
    return (lanczos_next, rows[:4, :64], gradient_product)


def solution(mesh):
    return jax.shard_map(
        on_device,
        mesh=mesh,
        in_specs=(
            P(None, ("row", "col")),
            P(("row", "col"), None),
            P(("row", "col")),
            P(),
            P(None, None, ("row", "col")),
            P(None, ("row", "col")),
            P("row", "col", None),
            P("row", "col", None),
        ),
        out_specs=(P(None, ("row", "col")), P(), P(None, ("row", "col"))),
        check_vma=False,
    )
```

```python
import functools
import math

import jax
import jax.numpy as jnp
from jax import lax
from jax.experimental import pallas as pl
from jax.experimental.pallas import tpu as pltpu
from jax.sharding import PartitionSpec as P


BLOCK = 256
GROUP = 4

ROOT_THREE = math.sqrt(3.0)
SUPPORT = 3.0
EPSILON = 1e-06
KERNEL_UNIT = 27.0 / 20.0
SLOPE_UNIT = 27.0
F32 = jnp.float32
BF16 = jnp.bfloat16


def shift_y(v, s):
    return lax.ppermute(v, "col", [(i, (i + 4 * s) % 16) for i in range(16)])


def shift_x(v, s):
    return lax.ppermute(v, "row", [(i, (i + 2 * s) % 8) for i in range(8)])


def flip_core(v):
    return lax.ppermute(v, "col", [(i, i ^ 1) for i in range(16)])


def flip_z_lo(v):
    return lax.ppermute(v, "col", [(i, i ^ 2) for i in range(16)])


def flip_z_hi(v):
    return lax.ppermute(v, "row", [(i, i ^ 1) for i in range(8)])


def sum_everywhere(v):
    for axis, size, bits in (("col", 16, (1, 2, 4, 8)), ("row", 8, (1, 2, 4))):
        for bit in bits:
            other = lax.ppermute(v, axis, [(i, i ^ bit) for i in range(size)])
            v = v + other
    return v


def gather_points(v):
    rows, cols = v[None], v[None]
    for row_bit, col_bit in ((2, 1), (4, 2), (8, 4), (1, None)):
        more = lax.ppermute(rows, "col", [(i, i ^ row_bit) for i in range(16)])
        rows = jnp.concatenate([rows, more])
        if col_bit is not None:
            more = lax.ppermute(cols, "row", [(i, i ^ col_bit) for i in range(8)])
            cols = jnp.concatenate([cols, more])
    return rows, cols


def gather_row_group(v):
    pair = jnp.stack([v, flip_z_hi(v)])
    return [pair] + [shift_x(pair, s) for s in (1, 2, 3)]


def gather_col_group(v):
    pair = jnp.stack([v, flip_z_lo(v)])
    own = [pair] + [shift_y(pair, s) for s in (1, 2, 3)]
    return own + [flip_core(v) for v in own]


def split_three(v):
    high = v.astype(BF16).astype(F32)
    rest = v - high
    middle = rest.astype(BF16).astype(F32)
    return high, middle, rest - middle


def split_two(v):
    scaled = v * 65537.0
    high = scaled - (scaled - v)
    return high, v - high


def tile_kernel(row_at, col_at, row_points, col_points, scale, kern, slope, left, right):
    @pl.when(pl.program_id(0) == 0)
    def _():
        def features(points, is_left):
            scaled = points * scale[...]
            size = scaled.shape[1]
            norm = split_three(jnp.sum(scaled * scaled, axis=0, keepdims=True))
            one = jnp.ones((1, size), F32)
            none = jnp.zeros((2, size), F32)
            if is_left:
                high, middle, low = split_three(scaled)
                parts = [high, high, middle, middle, high, low, *norm, one, one, one]
            else:
                high, middle, low = split_three(-2.0 * scaled)
                parts = [high, middle, high, middle, low, high, one, one, one, *norm]
            parts += [none, jnp.zeros((8, size), F32)]
            return jnp.concatenate(parts, axis=0).astype(BF16)

        width = row_points.shape[2]
        for held, points in ((left, row_points), (right, col_points)):
            for k in range(points.shape[0]):
                held[:, pl.ds(k * width, width)] = features(points[k], held is left)

    base = pl.program_id(0) * GROUP
    for g in range(GROUP):
        row_lane = pl.multiple_of(row_at[base + g], BLOCK)
        col_lane = pl.multiple_of(col_at[base + g], BLOCK)
        dist_sq = lax.dot_general(
            left[:, pl.ds(row_lane, BLOCK)],
            right[:, pl.ds(col_lane, BLOCK)],
            (((0,), (0,)), ((), ())),
            preferred_element_type=F32,
        )
        shifted = jnp.maximum(dist_sq, 0.0) + EPSILON / (SUPPORT * SUPPORT)
        radius = shifted * lax.rsqrt(shifted)
        decaying = jnp.exp2(radius * (-ROOT_THREE * SUPPORT / math.log(2.0)))
        tapered = jnp.maximum(1.0 - radius, 0.0)
        common = decaying * (tapered * tapered * tapered)
        weight = tapered * (1.0 + 4.0 * radius)
        growing = 1.0 / KERNEL_UNIT + (ROOT_THREE * SUPPORT / KERNEL_UNIT) * radius
        kernel_tile = common * weight * growing
        slope_tile = shifted * common * (weight + growing)
        for out, tile in ((kern, kernel_tile), (slope, slope_tile)):
            high, low = split_two(tile)
            out[g, 0] = high.astype(BF16)
            out[g, 1] = low.astype(BF16)


def make_tiles(row_at, col_at, row_points, col_points, scale):
    tiles = row_at.shape[0]
    whole = lambda v: pl.BlockSpec(v.shape, lambda i, *_: (0,) * v.ndim)
    out_spec = pl.BlockSpec((GROUP, 2, BLOCK, BLOCK), lambda i, *_: (i, 0, 0, 0))
    out = jax.ShapeDtypeStruct((tiles, 2, BLOCK, BLOCK), BF16)
    return pl.pallas_call(
        tile_kernel,
        out_shape=(out, out),
        grid_spec=pltpu.PrefetchScalarGridSpec(
            num_scalar_prefetch=2,
            grid=(tiles // GROUP,),
            in_specs=[whole(row_points), whole(col_points), whole(scale)],
            out_specs=(out_spec, out_spec),
            scratch_shapes=[
                pltpu.VMEM((64, row_points.shape[0] * 1024), BF16),
                pltpu.VMEM((64, col_points.shape[0] * 1024), BF16),
            ],
        ),
        compiler_params=pltpu.CompilerParams(vmem_limit_bytes=48 << 20),
        cost_estimate=pl.CostEstimate(
            flops=tiles * 30 * BLOCK * BLOCK,
            bytes_accessed=tiles * 8 * BLOCK * BLOCK,
            transcendentals=tiles * 2 * BLOCK * BLOCK,
        ),
        name="make_tiles",
    )(row_at, col_at, row_points, col_points, scale)


def product_kernel(row_count, col_count, flat, index, tiles, *refs):
    row_in, refs = refs[:row_count], refs[row_count:]
    col_in, refs = refs[:col_count], refs[col_count:]
    outs, refs = refs[: 3 if flat else 6], refs[3 if flat else 6 :]
    tiles_here, row_held, col_held, row_total, col_total, arrived, left = refs

    def fetch(step):
        some = pl.ds(step * GROUP, GROUP)
        return pltpu.make_async_copy(tiles.at[some], tiles_here.at[some], arrived.at[step])

    steps = tiles.shape[0] // GROUP

    @pl.loop(0, steps)
    def _(step):
        fetch(step).start()

    def hold(held, arrays):
        slot = 0
        for array in arrays:
            if len(array.shape) == 3:
                pieces = [array.at[k] for k in range(array.shape[0])]
            else:
                pieces = [array.at[:, pl.ds(k * 1024, 1024)] for k in range(array.shape[1] // 1024)]
            for piece in pieces:
                value = piece[...] * (SLOPE_UNIT if flat else KERNEL_UNIT)
                high = value.astype(BF16)
                held[slot, 0:64] = high
                held[slot, 64:128] = (value - high.astype(F32)).astype(BF16)
                slot += 1

    hold(row_held, row_in)
    hold(col_held, col_in)
    row_total[...] = jnp.zeros_like(row_total)
    col_total[...] = jnp.zeros_like(col_total)

    def times(values, tile_high, tile_low, contract):
        dims = (((1,), (contract,)), ((), ()))
        both = lax.dot_general(values, tile_high, dims, preferred_element_type=F32)
        low = lax.dot_general(values[:64], tile_low, dims, preferred_element_type=F32)
        return both[:64] + both[64:] + low

    @pl.loop(0, steps)
    def _(step):
        fetch(step).wait()
        for g in range(GROUP):
            t = step * GROUP + g
            row_lane = pl.ds(pl.multiple_of(index[4, t], BLOCK), BLOCK)
            col_lane = pl.ds(pl.multiple_of(index[5, t], BLOCK), BLOCK)
            mirror = index[6, t].astype(F32)
            high, low = tiles_here[t, 0], tiles_here[t, 1]
            direct = times(col_held[index[1, t], :, col_lane], high, low, 1)
            mirrored = times(row_held[index[0, t], :, row_lane], high, low, 0)
            row_total[index[2, t], :, row_lane] += direct
            col_total[index[3, t], :, col_lane] += mirrored * mirror

    if flat:
        slots = [row_total.at[k] for k in range(16)] + [col_total.at[k] for k in range(8)]
        places = [out.at[:, pl.ds(k * 1024, 1024)] for out in outs for k in range(8)]
    else:
        slots = [row_total.at[pl.ds(k * 8, 8)] for k in (0, 1)]
        slots += [col_total.at[pl.ds(k * 2, 2)] for k in range(4)]
        places = outs
    copies = [
        pltpu.make_async_copy(slot, place, left.at[k])
        for k, (slot, place) in enumerate(zip(slots, places))
    ]
    for copy in copies:
        copy.start()
    for copy in copies:
        copy.wait()


def products(index, tiles, row_in, col_in, flat):
    count = tiles.shape[0]
    here = pl.BlockSpec(memory_space=pltpu.VMEM)
    if flat:
        outs = [jax.ShapeDtypeStruct((64, 8 * 1024), F32)] * 3
    else:
        outs = [jax.ShapeDtypeStruct((8, 64, 1024), F32)] * 2
        outs += [jax.ShapeDtypeStruct((2, 64, 1024), F32)] * 4
    return pl.pallas_call(
        functools.partial(product_kernel, len(row_in), len(col_in), flat),
        out_shape=tuple(outs),
        in_specs=[pl.BlockSpec(memory_space=pltpu.SMEM), pl.BlockSpec(memory_space=pltpu.HBM)]
        + [here] * (len(row_in) + len(col_in)),
        out_specs=tuple(pl.BlockSpec(memory_space=pltpu.HBM) for _ in outs),
        scratch_shapes=[
            pltpu.VMEM(tiles.shape, BF16),
            pltpu.VMEM((16, 128, 1024), BF16),
            pltpu.VMEM((8, 128, 1024), BF16),
            pltpu.VMEM((16, 64, 1024), F32),
            pltpu.VMEM((8, 64, 1024), F32),
            pltpu.SemaphoreType.DMA((count // GROUP,)),
            pltpu.SemaphoreType.DMA((24,)),
        ],
        compiler_params=pltpu.CompilerParams(vmem_limit_bytes=60_200_000),
        cost_estimate=pl.CostEstimate(
            flops=count * 12 * 64 * BLOCK * BLOCK,
            bytes_accessed=count * 4 * BLOCK * BLOCK + (12 << 20),
            transcendentals=0,
        ),
        name="slope_products" if flat else "kernel_products",
    )(index, tiles, *row_in, *col_in)


def column_sums(pairs, columns):
    lane = lax.broadcasted_iota(jnp.int32, (8, columns), 1)
    held = jnp.zeros((8, columns), F32)
    for k, (a, b) in enumerate(pairs):
        held = jnp.where(lane == k, jnp.sum(a * b, axis=1, keepdims=True), held)
    return held


def row_blocks_of(rows):
    return lambda body: pl.loop(0, rows // 8)(
        lambda step: body(pl.ds(pl.multiple_of(step * 8, 8), 8))
    )


def vectors_at(earlier, extra, at):
    return [earlier[h, at] for h in range(earlier.shape[0])] + [v[at] for v in extra]


def dots_kernel(piece_count, extra_count, earlier, noise, *refs):
    pieces, refs = refs[:piece_count], refs[piece_count:]
    extra, (image_out, dots_out, held) = refs[:extra_count], refs[extra_count:]
    held[...] = jnp.zeros_like(held)

    @row_blocks_of(image_out.shape[0])
    def _(at):
        image = noise[...] * extra[-1][at]
        for piece in pieces:
            if len(piece.shape) == 3:
                image = image + piece[0, at]
            else:
                image = image + piece[at]
        image_out[at] = image
        vectors = vectors_at(earlier, extra, at) + [image]
        held[at] = column_sums([(v, image) for v in vectors], 128)

    dots_out[...] = held[...].T[: dots_out.shape[0]]


def image_dots(earlier, noise, pieces, extra):
    rows, lanes = extra[-1].shape
    return pl.pallas_call(
        functools.partial(dots_kernel, len(pieces), len(extra)),
        out_shape=(
            jax.ShapeDtypeStruct((rows, lanes), F32),
            jax.ShapeDtypeStruct((24, 128), F32),
        ),
        scratch_shapes=[pltpu.VMEM((128, 128), F32)],
        compiler_params=pltpu.CompilerParams(vmem_limit_bytes=2 << 20),
        cost_estimate=pl.CostEstimate(
            flops=rows * lanes * 60, bytes_accessed=rows * lanes * 4 * 30, transcendentals=0
        ),
        name="image_dots",
    )(earlier, noise, *pieces, *extra)


def gram_kernel(earlier, first, out, held):
    held[...] = jnp.zeros_like(held)

    @row_blocks_of(first.shape[0])
    def _(at):
        vectors = vectors_at(earlier, [first], at)
        count = len(vectors)
        pairs = [(vectors[i], vectors[i + d]) for d in range(count) for i in range(count - d)]
        held[at, 0:128] = column_sums(pairs[:128], 128)
        held[at, 128:256] = column_sums(pairs[128:], 128)

    out[0:128] = held[:, 0:128].T
    out[128:160] = held[:, 128:256].T[:32]


def gram_sums(earlier, first):
    rows, lanes = first.shape
    return pl.pallas_call(
        gram_kernel,
        out_shape=jax.ShapeDtypeStruct((160, 128), F32),
        scratch_shapes=[pltpu.VMEM((128, 256), F32)],
        compiler_params=pltpu.CompilerParams(vmem_limit_bytes=2 << 20),
        cost_estimate=pl.CostEstimate(
            flops=rows * lanes * 400, bytes_accessed=rows * lanes * 4 * 18, transcendentals=0
        ),
        name="gram_sums",
    )(earlier, first)


def turned(values):
    rows = values.shape[0]
    return jnp.concatenate([values, jnp.zeros((128 - rows, 128), F32)], axis=0).T


def combine(columns, image, vectors):
    total = columns[:, 0:1] * image
    for k, v in enumerate(vectors):
        total = total - columns[:, k + 1 : k + 2] * v
    return total


def first_rest_kernel(total, sums, image, earlier, first, rest, held):
    means = sums[0:17] * (1.0 / total)
    held[...] = turned(jnp.concatenate([jnp.ones((1, 128), F32), means], axis=0))

    @row_blocks_of(rest.shape[0])
    def _(at):
        rest[at] = combine(held[at], image[at], vectors_at(earlier, [first], at))


def last_rest_kernel(
    total, sums, next_sums, gram, image, earlier, first, second, out, coefficients, held, here, moved
):
    blocks = here.shape[1] // 8

    def fetch(k):
        at = pl.ds(k * 8, 8)
        return pltpu.make_async_copy(earlier.at[:, at], here.at[:, at], moved.at[k])

    for k in range(blocks):
        fetch(k).start()
    count = 17
    means = sums[...] * (1.0 / total)
    along = means[0:count]
    turned_along = jnp.zeros((count, 128), F32)
    at = 0
    diagonals = []
    for d in range(count):
        size = count - d
        diagonal = gram[at : at + size] * (1.0 / total)
        diagonals.append(diagonal)
        part = diagonal * along[d:]
        if d:
            other = diagonal * along[:size]
            blank = jnp.zeros((d, 128), F32)
            part = jnp.concatenate([part, blank], axis=0) + jnp.concatenate([blank, other], axis=0)
        turned_along = turned_along + part
        at += size
    rest_means = along - turned_along
    column = lambda v: jnp.sum(v, axis=0, keepdims=True)
    norm = means[17:18] - 2.0 * column(along * along) + column(along * turned_along)
    norm = jnp.maximum(norm, 0.0)
    norm_sq = norm + EPSILON
    scale = 1.0 / jnp.sqrt(norm_sq)

    next_means = next_sums[...] * (1.0 / total)
    next_along = next_means[0:count] * scale
    alpha = next_means[17:18] * (scale * scale)
    beside = alpha * scale
    rest_sq = (
        next_means[18:19] * (scale * scale)
        - 2.0 * (column(next_along * next_along) + alpha * alpha)
        + 2.0 * beside * column(next_along * rest_means)
        + beside * beside * norm
    )
    for d in range(count):
        part = column(next_along[: count - d] * next_along[d:] * diagonals[d])
        rest_sq = rest_sq + (1.0 if d == 0 else 2.0) * part
    beta = jnp.sqrt(jnp.maximum(rest_sq, 0.0) + EPSILON)
    held[...] = turned(jnp.concatenate([scale, next_along, beside], axis=0) / beta)
    coefficients[...] = jnp.concatenate(
        [along[16:17], jnp.sqrt(norm_sq), alpha, beta, jnp.zeros((4, 128), F32)], axis=0
    )

    @pl.loop(0, blocks)
    def _(k):
        fetch(k).wait()
        at = pl.ds(pl.multiple_of(k * 8, 8), 8)
        out[at] = combine(held[at], image[at], vectors_at(here, [first, second], at))


def rest_call(kernel, total, smalls, image, earlier, extra, with_coefficients):
    rows, lanes = image.shape
    out_shape = [jax.ShapeDtypeStruct((rows, lanes), F32)]
    near = pl.BlockSpec(memory_space=pltpu.VMEM)
    scratch = [pltpu.VMEM((128, 128), F32)]
    if with_coefficients:
        out_shape.append(jax.ShapeDtypeStruct((8, 128), F32))
        scratch += [pltpu.VMEM(earlier.shape, F32), pltpu.SemaphoreType.DMA((rows // 8,))]
    return pl.pallas_call(
        functools.partial(kernel, float(total)),
        out_shape=tuple(out_shape),
        in_specs=[near] * (len(smalls) + 1)
        + [pl.BlockSpec(memory_space=pltpu.HBM) if with_coefficients else near]
        + [near] * len(extra),
        scratch_shapes=scratch,
        compiler_params=pltpu.CompilerParams(vmem_limit_bytes=8 << 20),
        cost_estimate=pl.CostEstimate(
            flops=rows * lanes * 40, bytes_accessed=rows * lanes * 4 * 20, transcendentals=0
        ),
    )(*smalls, image, earlier, *extra)


def reduce_parts(parts):
    row_keep, row_send, cols = parts[0], parts[1], parts[2:]
    row_got = flip_core(row_send)
    col_got = []
    for s in (2, 1, 3):
        col_got.append(shift_x(cols[s], s))
    own = [row_keep[2 * s : 2 * s + 2] + row_got[2 * s : 2 * s + 2] for s in range(4)]
    row_got = []
    for s in (2, 1, 3):
        row_got.append(shift_y(own[s], s))
    col_sum = cols[0] + col_got[0] + col_got[1] + col_got[2]
    row_sum = own[0] + row_got[0] + row_got[1] + row_got[2]
    return [col_sum, row_sum, flip_z_hi(col_sum[1]), flip_z_lo(row_sum[1])]


def on_device(
    points, point_order, noise_var, inv_scale, basis_vectors, current, tile_rows, tile_cols
):
    per_device = points.shape[1]
    row_at = lax.axis_index("row")
    col_at = lax.axis_index("col")
    point_total = per_device * 128
    arrangement = point_order[0]
    arranged = jnp.take(points, arrangement, axis=1)
    noise_here = jnp.take(noise_var, arrangement)
    row_blocks = tile_rows[0, 0]
    col_blocks = tile_cols[0, 0]
    row_owner, row_sub = row_blocks // 4, row_blocks % 4
    col_owner, col_sub = col_blocks // 4, col_blocks % 4
    mirror = ((row_at * 16 + row_owner) * 4 + row_sub) != (
        (col_owner * 16 + col_at) * 4 + col_sub
    )
    core_rel = (row_owner ^ col_at) & 1
    zlo_rel = ((row_owner ^ col_at) >> 1) & 1
    y_to = (row_owner // 4 - col_at // 4) & 3
    zhi_rel = (col_owner ^ row_at) & 1
    x_to = (col_owner // 2 - row_at // 2) & 3
    row_from = core_rel * 8 + ((4 - y_to) & 3) * 2 + zlo_rel
    row_to = core_rel * 8 + y_to * 2 + zlo_rel
    col_from = ((4 - x_to) & 3) * 2 + zhi_rel
    col_to = x_to * 2 + zhi_rel

    def table(row_in, col_in, row_out, col_out):
        rows = [row_in, col_in, row_out, col_out, row_sub * BLOCK, col_sub * BLOCK, mirror]
        return jnp.stack([v.astype(jnp.int32) for v in rows])

    row_points, col_points = gather_points(arranged)
    row_xor, col_xor = row_owner ^ col_at, col_owner ^ row_at
    kern, slope = make_tiles(
        ((row_xor & 1) * 8 + (row_xor >> 1)) * 1024 + row_sub * BLOCK,
        col_xor * 1024 + col_sub * BLOCK,
        row_points,
        col_points,
        inv_scale[:, None] * (1.0 / SUPPORT),
    )

    noise = noise_here[None]
    row_in = [lax.all_gather(current, "col", axis=1, tiled=True)]
    kern, current_later = lax.optimization_barrier((kern, current))
    first_table = table(row_owner, col_from, row_to, col_to)
    gram, first_table = lax.optimization_barrier(
        (gram_sums(basis_vectors, current_later), first_table)
    )
    gram = lax.psum(gram, ("row", "col"))
    col_in = gather_row_group(current)
    parts = products(first_table, kern, row_in, col_in, False)
    pieces = reduce_parts(parts)
    slope_to = core_rel * 8 + (row_owner >> 1)
    row_keep, row_send, col_part = products(
        table(row_owner, col_from, slope_to, col_owner), slope, row_in, col_in, True
    )
    col_sum = lax.psum_scatter(col_part, "row", scatter_dimension=1, tiled=True)
    row_part = row_keep + flip_core(row_send)
    row_sum = lax.psum_scatter(
        row_part,
        "col",
        scatter_dimension=1,
        tiled=True,
        axis_index_groups=[[i * 2 + core for i in range(8)] for core in range(2)],
    )
    gradient_product = row_sum + col_sum
    image, sums = image_dots(basis_vectors, noise, pieces, [current])
    sums = sum_everywhere(sums)
    (rest,) = rest_call(
        first_rest_kernel, point_total, [sums], image, basis_vectors, [current], False
    )

    row_in = gather_col_group(rest)
    col_in = gather_row_group(rest)
    parts = products(table(row_from, col_from, row_to, col_to), kern, row_in, col_in, False)
    pieces = reduce_parts(parts)
    image, next_sums = image_dots(basis_vectors, noise, pieces, [current, rest])
    next_sums = sum_everywhere(next_sums)
    lanczos_next, rows = rest_call(
        last_rest_kernel,
        point_total,
        [sums, next_sums, gram],
        image,
        basis_vectors,
        [current, rest],
        True,
    )
    return (lanczos_next, rows[:4, :64], gradient_product)


def solution(mesh):
    return jax.shard_map(
        on_device,
        mesh=mesh,
        in_specs=(
            P(None, ("row", "col")),
            P(("row", "col"), None),
            P(("row", "col")),
            P(),
            P(None, None, ("row", "col")),
            P(None, ("row", "col")),
            P("row", "col", None),
            P("row", "col", None),
        ),
        out_specs=(P(None, ("row", "col")), P(), P(None, ("row", "col"))),
        check_vma=False,
    )
```

```python
import functools
import math

import jax
import jax.numpy as jnp
from jax import lax
from jax.experimental import pallas as pl
from jax.experimental.pallas import tpu as pltpu
from jax.sharding import PartitionSpec as P


BLOCK = 256
GROUP = 4

ROOT_THREE = math.sqrt(3.0)
SUPPORT = 3.0
EPSILON = 1e-06
F32 = jnp.float32
BF16 = jnp.bfloat16


def shift_y(v, s):
    return lax.ppermute(v, "col", [(i, (i + 4 * s) % 16) for i in range(16)])


def shift_x(v, s):
    return lax.ppermute(v, "row", [(i, (i + 2 * s) % 8) for i in range(8)])


def flip_core(v):
    return lax.ppermute(v, "col", [(i, i ^ 1) for i in range(16)])


def flip_z_lo(v):
    return lax.ppermute(v, "col", [(i, i ^ 2) for i in range(16)])


def flip_z_hi(v):
    return lax.ppermute(v, "row", [(i, i ^ 1) for i in range(8)])


def sum_everywhere(v):
    for axis, size, bits in (("col", 16, (1, 2, 4, 8)), ("row", 8, (1, 2, 4))):
        for bit in bits:
            v = v + lax.ppermute(v, axis, [(i, i ^ bit) for i in range(size)])
    return v


def gather_points(v):
    rows, cols = v[None], v[None]
    for row_bit, col_bit in ((2, 1), (4, 2), (8, 4), (1, None)):
        more = lax.ppermute(rows, "col", [(i, i ^ row_bit) for i in range(16)])
        rows = jnp.concatenate([rows, more])
        if col_bit is not None:
            more = lax.ppermute(cols, "row", [(i, i ^ col_bit) for i in range(8)])
            cols = jnp.concatenate([cols, more])
    return rows, cols


def gather_row_group(v):
    pair = jnp.stack([v, flip_z_hi(v)])
    return [pair] + [shift_x(pair, s) for s in (1, 2, 3)]


def gather_col_group(v):
    pair = jnp.stack([v, flip_z_lo(v)])
    own = [pair] + [shift_y(pair, s) for s in (1, 2, 3)]
    return own + [flip_core(v) for v in own]


def split_three(v):
    high = v.astype(BF16).astype(F32)
    rest = v - high
    middle = rest.astype(BF16).astype(F32)
    return high, middle, rest - middle


def split_two(v):
    scaled = v * 65537.0
    high = scaled - (scaled - v)
    return high, v - high


def tile_kernel(row_at, col_at, row_points, col_points, scale, kern, slope, left, right):
    @pl.when(pl.program_id(0) == 0)
    def _():
        def features(points, is_left):
            scaled = points * scale[...]
            size = scaled.shape[1]
            norm = split_three(jnp.sum(scaled * scaled, axis=0, keepdims=True))
            one = jnp.ones((1, size), F32)
            none = jnp.zeros((2, size), F32)
            if is_left:
                high, middle, low = split_three(scaled)
                parts = [high, high, middle, middle, high, low, *norm, one, one, one]
            else:
                high, middle, low = split_three(-2.0 * scaled)
                parts = [high, middle, high, middle, low, high, one, one, one, *norm]
            parts += [none, jnp.zeros((8, size), F32)]
            return jnp.concatenate(parts, axis=0).astype(BF16)

        width = row_points.shape[2]
        for held, points in ((left, row_points), (right, col_points)):
            for k in range(points.shape[0]):
                held[:, pl.ds(k * width, width)] = features(points[k], held is left)

    base = pl.program_id(0) * GROUP
    for g in range(GROUP):
        row_lane = pl.multiple_of(row_at[base + g], BLOCK)
        col_lane = pl.multiple_of(col_at[base + g], BLOCK)
        dist_sq = lax.dot_general(
            left[:, pl.ds(row_lane, BLOCK)],
            right[:, pl.ds(col_lane, BLOCK)],
            (((0,), (0,)), ((), ())),
            preferred_element_type=F32,
        )
        shifted = jnp.maximum(dist_sq, 0.0) + EPSILON
        radius = shifted * lax.rsqrt(shifted)
        decaying = jnp.exp2(radius * (-ROOT_THREE / math.log(2.0)))
        tapered = jnp.maximum(1.0 - radius * (1.0 / SUPPORT), 0.0)
        common = decaying * (tapered * tapered * tapered)
        weight = tapered * (3.0 + (12.0 / SUPPORT) * radius)
        growing = (1.0 / 3.0) + (ROOT_THREE / 3.0) * radius
        kernel_tile = common * weight * growing
        slope_tile = shifted * common * (weight + (60.0 / (SUPPORT * SUPPORT)) * growing)
        for out, tile in ((kern, kernel_tile), (slope, slope_tile)):
            high, low = split_two(tile)
            out[g, 0] = high.astype(BF16)
            out[g, 1] = low.astype(BF16)


def make_tiles(row_at, col_at, row_points, col_points, scale):
    tiles = row_at.shape[0]
    whole = lambda v: pl.BlockSpec(v.shape, lambda i, *_: (0,) * v.ndim)
    out_spec = pl.BlockSpec((GROUP, 2, BLOCK, BLOCK), lambda i, *_: (i, 0, 0, 0))
    out = jax.ShapeDtypeStruct((tiles, 2, BLOCK, BLOCK), BF16)
    return pl.pallas_call(
        tile_kernel,
        out_shape=(out, out),
        grid_spec=pltpu.PrefetchScalarGridSpec(
            num_scalar_prefetch=2,
            grid=(tiles // GROUP,),
            in_specs=[whole(row_points), whole(col_points), whole(scale)],
            out_specs=(out_spec, out_spec),
            scratch_shapes=[
                pltpu.VMEM((64, row_points.shape[0] * 1024), BF16),
                pltpu.VMEM((64, col_points.shape[0] * 1024), BF16),
            ],
        ),
        compiler_params=pltpu.CompilerParams(vmem_limit_bytes=48 << 20),
        cost_estimate=pl.CostEstimate(
            flops=tiles * 30 * BLOCK * BLOCK,
            bytes_accessed=tiles * 8 * BLOCK * BLOCK,
            transcendentals=tiles * 2 * BLOCK * BLOCK,
        ),
        name="make_tiles",
    )(row_at, col_at, row_points, col_points, scale)


def product_kernel(row_count, col_count, flat, index, tiles, *refs):
    row_in, refs = refs[:row_count], refs[row_count:]
    col_in, refs = refs[:col_count], refs[col_count:]
    outs, refs = refs[: 3 if flat else 6], refs[3 if flat else 6 :]
    tiles_here, row_held, col_held, row_total, col_total, arrived, left = refs

    def fetch(step):
        some = pl.ds(step * GROUP, GROUP)
        return pltpu.make_async_copy(tiles.at[some], tiles_here.at[some], arrived.at[step])

    steps = tiles.shape[0] // GROUP

    @pl.loop(0, steps)
    def _(step):
        fetch(step).start()

    def hold(held, arrays):
        slot = 0
        for array in arrays:
            if len(array.shape) == 3:
                pieces = [array.at[k] for k in range(array.shape[0])]
            else:
                pieces = [array.at[:, pl.ds(k * 1024, 1024)] for k in range(array.shape[1] // 1024)]
            for piece in pieces:
                value = piece[...]
                high = value.astype(BF16)
                held[slot, 0:64] = high
                held[slot, 64:128] = (value - high.astype(F32)).astype(BF16)
                slot += 1

    hold(row_held, row_in)
    hold(col_held, col_in)
    row_total[...] = jnp.zeros_like(row_total)
    col_total[...] = jnp.zeros_like(col_total)

    def times(values, tile_high, tile_low, contract):
        dims = (((1,), (contract,)), ((), ()))
        both = lax.dot_general(values, tile_high, dims, preferred_element_type=F32)
        low = lax.dot_general(values[:64], tile_low, dims, preferred_element_type=F32)
        return both[:64] + both[64:] + low

    @pl.loop(0, steps)
    def _(step):
        fetch(step).wait()
        for g in range(GROUP):
            t = step * GROUP + g
            row_lane = pl.ds(pl.multiple_of(index[4, t], BLOCK), BLOCK)
            col_lane = pl.ds(pl.multiple_of(index[5, t], BLOCK), BLOCK)
            mirror = index[6, t].astype(F32)
            high, low = tiles_here[t, 0], tiles_here[t, 1]
            direct = times(col_held[index[1, t], :, col_lane], high, low, 1)
            mirrored = times(row_held[index[0, t], :, row_lane], high, low, 0)
            row_total[index[2, t], :, row_lane] += direct
            col_total[index[3, t], :, col_lane] += mirrored * mirror

    if flat:
        slots = [row_total.at[k] for k in range(16)] + [col_total.at[k] for k in range(8)]
        places = [out.at[:, pl.ds(k * 1024, 1024)] for out in outs for k in range(8)]
    else:
        slots = [row_total.at[pl.ds(k * 8, 8)] for k in (0, 1)]
        slots += [col_total.at[pl.ds(k * 2, 2)] for k in range(4)]
        places = outs
    copies = [
        pltpu.make_async_copy(slot, place, left.at[k])
        for k, (slot, place) in enumerate(zip(slots, places))
    ]
    for copy in copies:
        copy.start()
    for copy in copies:
        copy.wait()


def products(index, tiles, row_in, col_in, flat):
    count = tiles.shape[0]
    here = pl.BlockSpec(memory_space=pltpu.VMEM)
    if flat:
        outs = [jax.ShapeDtypeStruct((64, 8 * 1024), F32)] * 3
    else:
        outs = [jax.ShapeDtypeStruct((8, 64, 1024), F32)] * 2
        outs += [jax.ShapeDtypeStruct((2, 64, 1024), F32)] * 4
    return pl.pallas_call(
        functools.partial(product_kernel, len(row_in), len(col_in), flat),
        out_shape=tuple(outs),
        in_specs=[pl.BlockSpec(memory_space=pltpu.SMEM), pl.BlockSpec(memory_space=pltpu.HBM)]
        + [here] * (len(row_in) + len(col_in)),
        out_specs=tuple(pl.BlockSpec(memory_space=pltpu.HBM) for _ in outs),
        scratch_shapes=[
            pltpu.VMEM(tiles.shape, BF16),
            pltpu.VMEM((16, 128, 1024), BF16),
            pltpu.VMEM((8, 128, 1024), BF16),
            pltpu.VMEM((16, 64, 1024), F32),
            pltpu.VMEM((8, 64, 1024), F32),
            pltpu.SemaphoreType.DMA((count // GROUP,)),
            pltpu.SemaphoreType.DMA((24,)),
        ],
        compiler_params=pltpu.CompilerParams(vmem_limit_bytes=60_200_000),
        cost_estimate=pl.CostEstimate(
            flops=count * 12 * 64 * BLOCK * BLOCK,
            bytes_accessed=count * 4 * BLOCK * BLOCK + (12 << 20),
            transcendentals=0,
        ),
        name="slope_products" if flat else "kernel_products",
    )(index, tiles, *row_in, *col_in)


def column_sums(pairs, columns):
    lane = lax.broadcasted_iota(jnp.int32, (8, columns), 1)
    held = jnp.zeros((8, columns), F32)
    for k, (a, b) in enumerate(pairs):
        held = jnp.where(lane == k, jnp.sum(a * b, axis=1, keepdims=True), held)
    return held


def row_blocks_of(rows):
    return lambda body: pl.loop(0, rows // 8)(
        lambda step: body(pl.ds(pl.multiple_of(step * 8, 8), 8))
    )


def vectors_at(earlier, extra, at):
    return [earlier[h, at] for h in range(earlier.shape[0])] + [v[at] for v in extra]


def dots_kernel(piece_count, extra_count, earlier, noise, *refs):
    pieces, refs = refs[:piece_count], refs[piece_count:]
    extra, (image_out, dots_out, held) = refs[:extra_count], refs[extra_count:]
    held[...] = jnp.zeros_like(held)

    @row_blocks_of(image_out.shape[0])
    def _(at):
        image = noise[...] * extra[-1][at]
        for piece in pieces:
            if len(piece.shape) == 3:
                image = image + piece[0, at]
            else:
                image = image + piece[at]
        image_out[at] = image
        vectors = vectors_at(earlier, extra, at) + [image]
        held[at] = column_sums([(v, image) for v in vectors], 128)

    dots_out[...] = held[...].T[: dots_out.shape[0]]


def image_dots(earlier, noise, pieces, extra):
    rows, lanes = extra[-1].shape
    return pl.pallas_call(
        functools.partial(dots_kernel, len(pieces), len(extra)),
        out_shape=(
            jax.ShapeDtypeStruct((rows, lanes), F32),
            jax.ShapeDtypeStruct((24, 128), F32),
        ),
        scratch_shapes=[pltpu.VMEM((128, 128), F32)],
        compiler_params=pltpu.CompilerParams(vmem_limit_bytes=2 << 20),
        cost_estimate=pl.CostEstimate(
            flops=rows * lanes * 60, bytes_accessed=rows * lanes * 4 * 30, transcendentals=0
        ),
        name="image_dots",
    )(earlier, noise, *pieces, *extra)


def gram_kernel(earlier, first, out, held):
    held[...] = jnp.zeros_like(held)

    @row_blocks_of(first.shape[0])
    def _(at):
        vectors = vectors_at(earlier, [first], at)
        count = len(vectors)
        pairs = [(vectors[i], vectors[i + d]) for d in range(count) for i in range(count - d)]
        held[at, 0:128] = column_sums(pairs[:128], 128)
        held[at, 128:256] = column_sums(pairs[128:], 128)

    out[0:128] = held[:, 0:128].T
    out[128:160] = held[:, 128:256].T[:32]


def gram_sums(earlier, first):
    rows, lanes = first.shape
    return pl.pallas_call(
        gram_kernel,
        out_shape=jax.ShapeDtypeStruct((160, 128), F32),
        scratch_shapes=[pltpu.VMEM((128, 256), F32)],
        compiler_params=pltpu.CompilerParams(vmem_limit_bytes=2 << 20),
        cost_estimate=pl.CostEstimate(
            flops=rows * lanes * 400, bytes_accessed=rows * lanes * 4 * 18, transcendentals=0
        ),
        name="gram_sums",
    )(earlier, first)


def turned(values):
    rows = values.shape[0]
    return jnp.concatenate([values, jnp.zeros((128 - rows, 128), F32)], axis=0).T


def combine(columns, image, vectors):
    total = columns[:, 0:1] * image
    for k, v in enumerate(vectors):
        total = total - columns[:, k + 1 : k + 2] * v
    return total


def first_rest_kernel(total, sums, image, earlier, first, rest, held):
    means = sums[0:17] * (1.0 / total)
    held[...] = turned(jnp.concatenate([jnp.ones((1, 128), F32), means], axis=0))

    @row_blocks_of(rest.shape[0])
    def _(at):
        rest[at] = combine(held[at], image[at], vectors_at(earlier, [first], at))


def last_rest_kernel(
    total, sums, next_sums, gram, image, earlier, first, second, out, coefficients, held
):
    count = 17
    means = sums[...] * (1.0 / total)
    along = means[0:count]
    turned_along = jnp.zeros((count, 128), F32)
    at = 0
    diagonals = []
    for d in range(count):
        size = count - d
        diagonal = gram[at : at + size] * (1.0 / total)
        diagonals.append(diagonal)
        part = diagonal * along[d:]
        if d:
            other = diagonal * along[:size]
            blank = jnp.zeros((d, 128), F32)
            part = jnp.concatenate([part, blank], axis=0) + jnp.concatenate([blank, other], axis=0)
        turned_along = turned_along + part
        at += size
    rest_means = along - turned_along
    column = lambda v: jnp.sum(v, axis=0, keepdims=True)
    norm = means[17:18] - 2.0 * column(along * along) + column(along * turned_along)
    norm = jnp.maximum(norm, 0.0)
    norm_sq = norm + EPSILON
    scale = 1.0 / jnp.sqrt(norm_sq)

    next_means = next_sums[...] * (1.0 / total)
    next_along = next_means[0:count] * scale
    alpha = next_means[17:18] * (scale * scale)
    beside = alpha * scale
    rest_sq = (
        next_means[18:19] * (scale * scale)
        - 2.0 * (column(next_along * next_along) + alpha * alpha)
        + 2.0 * beside * column(next_along * rest_means)
        + beside * beside * norm
    )
    for d in range(count):
        part = column(next_along[: count - d] * next_along[d:] * diagonals[d])
        rest_sq = rest_sq + (1.0 if d == 0 else 2.0) * part
    beta = jnp.sqrt(jnp.maximum(rest_sq, 0.0) + EPSILON)
    held[...] = turned(jnp.concatenate([scale, next_along, beside], axis=0) / beta)
    coefficients[...] = jnp.concatenate(
        [along[16:17], jnp.sqrt(norm_sq), alpha, beta], axis=0
    )[:, :64]

    @row_blocks_of(out.shape[0])
    def _(at):
        out[at] = combine(held[at], image[at], vectors_at(earlier, [first, second], at))


def rest_call(kernel, total, smalls, image, earlier, extra, with_coefficients):
    rows, lanes = image.shape
    out_shape = [jax.ShapeDtypeStruct((rows, lanes), F32)]
    if with_coefficients:
        out_shape.append(jax.ShapeDtypeStruct((4, 64), F32))
    return pl.pallas_call(
        functools.partial(kernel, float(total)),
        out_shape=tuple(out_shape),
        scratch_shapes=[pltpu.VMEM((128, 128), F32)],
        compiler_params=pltpu.CompilerParams(vmem_limit_bytes=2 << 20),
        cost_estimate=pl.CostEstimate(
            flops=rows * lanes * 40, bytes_accessed=rows * lanes * 4 * 20, transcendentals=0
        ),
    )(*smalls, image, earlier, *extra)


def reduce_parts(parts):
    row_keep, row_send, cols = parts[0], parts[1], parts[2:]
    row_got = flip_core(row_send)
    col_got = []
    for s in (2, 1, 3):
        col_got.append(shift_x(cols[s], s))
    own = [row_keep[2 * s : 2 * s + 2] + row_got[2 * s : 2 * s + 2] for s in range(4)]
    row_got = []
    for s in (2, 1, 3):
        row_got.append(shift_y(own[s], s))
    col_sum = cols[0] + col_got[0] + col_got[1] + col_got[2]
    row_sum = own[0] + row_got[0] + row_got[1] + row_got[2]
    return [col_sum, row_sum, flip_z_hi(col_sum[1]), flip_z_lo(row_sum[1])]


def on_device(
    points, point_order, noise_var, inv_scale, basis_vectors, current, tile_rows, tile_cols
):
    per_device = points.shape[1]
    row_at = lax.axis_index("row")
    col_at = lax.axis_index("col")
    point_total = per_device * 128
    arrangement = point_order[0]
    arranged = jnp.take(points, arrangement, axis=1)
    noise_here = jnp.take(noise_var, arrangement)
    row_blocks = tile_rows[0, 0]
    col_blocks = tile_cols[0, 0]
    row_owner, row_sub = row_blocks // 4, row_blocks % 4
    col_owner, col_sub = col_blocks // 4, col_blocks % 4
    mirror = ((row_at * 16 + row_owner) * 4 + row_sub) != (
        (col_owner * 16 + col_at) * 4 + col_sub
    )
    core_rel = (row_owner ^ col_at) & 1
    zlo_rel = ((row_owner ^ col_at) >> 1) & 1
    y_to = (row_owner // 4 - col_at // 4) & 3
    zhi_rel = (col_owner ^ row_at) & 1
    x_to = (col_owner // 2 - row_at // 2) & 3
    row_from = core_rel * 8 + ((4 - y_to) & 3) * 2 + zlo_rel
    row_to = core_rel * 8 + y_to * 2 + zlo_rel
    col_from = ((4 - x_to) & 3) * 2 + zhi_rel
    col_to = x_to * 2 + zhi_rel

    def table(row_in, col_in, row_out, col_out):
        rows = [row_in, col_in, row_out, col_out, row_sub * BLOCK, col_sub * BLOCK, mirror]
        return jnp.stack([v.astype(jnp.int32) for v in rows])

    row_points, col_points = gather_points(arranged)
    row_xor, col_xor = row_owner ^ col_at, col_owner ^ row_at
    slope_to = core_rel * 8 + (row_owner >> 1)
    row_points, slope_table, next_table = lax.optimization_barrier(
        (
            row_points,
            table(row_owner, col_from, slope_to, col_owner),
            table(row_from, col_from, row_to, col_to),
        )
    )
    kern, slope = make_tiles(
        ((row_xor & 1) * 8 + (row_xor >> 1)) * 1024 + row_sub * BLOCK,
        col_xor * 1024 + col_sub * BLOCK,
        row_points,
        col_points,
        inv_scale[:, None],
    )

    noise = noise_here[None]
    row_in = [lax.all_gather(current, "col", axis=1, tiled=True)]
    kern, current_later = lax.optimization_barrier((kern, current))
    first_table = table(row_owner, col_from, row_to, col_to)
    gram, first_table = lax.optimization_barrier(
        (gram_sums(basis_vectors, current_later), first_table)
    )
    gram = lax.psum(gram, ("row", "col"))
    col_in = gather_row_group(current)
    parts = products(first_table, kern, row_in, col_in, False)
    pieces = reduce_parts(parts)
    row_keep, row_send, col_part = products(
        slope_table, slope, row_in, col_in, True
    )
    col_sum = lax.psum_scatter(col_part, "row", scatter_dimension=1, tiled=True)
    row_part = row_keep + flip_core(row_send)
    row_sum = lax.psum_scatter(
        row_part,
        "col",
        scatter_dimension=1,
        tiled=True,
        axis_index_groups=[[i * 2 + core for i in range(8)] for core in range(2)],
    )
    gradient_product = row_sum + col_sum
    image, sums = image_dots(basis_vectors, noise, pieces, [current])
    sums = sum_everywhere(sums)
    (rest,) = rest_call(
        first_rest_kernel, point_total, [sums], image, basis_vectors, [current], False
    )

    row_in = gather_col_group(rest)
    col_in = gather_row_group(rest)
    parts = products(next_table, kern, row_in, col_in, False)
    pieces = reduce_parts(parts)
    image, next_sums = image_dots(basis_vectors, noise, pieces, [current, rest])
    next_sums = sum_everywhere(next_sums)
    lanczos_next, rows = rest_call(
        last_rest_kernel,
        point_total,
        [sums, next_sums, gram],
        image,
        basis_vectors,
        [current, rest],
        True,
    )
    return (lanczos_next, rows, gradient_product)


def solution(mesh):
    return jax.shard_map(
        on_device,
        mesh=mesh,
        in_specs=(
            P(None, ("row", "col")),
            P(("row", "col"), None),
            P(("row", "col")),
            P(),
            P(None, None, ("row", "col")),
            P(None, ("row", "col")),
            P("row", "col", None),
            P("row", "col", None),
        ),
        out_specs=(P(None, ("row", "col")), P(), P(None, ("row", "col"))),
        check_vma=False,
    )
```
